256 devices in a mesh: mem: 32 (over y, z_lo, core), tile: 8 (over x, z_hi).
Axes of the slice: x: 4, y: 4, z: 8 (z_hi: 2, z_lo: 4; z = z_hi * 4 + z_lo), core: 2. Of those that a mesh axis runs over, the one named last changes fastest.
Arguments:
- weights: float32 [32, 8, 128, 512], P('mem', None, 'tile'), may hold values from -3 to 3
- perturb: bfloat16 [32, 8, 128, 512], P('mem', None, 'tile'), may hold values from -6 to 6
- coef_lon: float32 [8, 128, 512], P(None, 'tile'), may hold values from 0.01 to 0.09
- coef_lat: float32 [8, 128, 512], P(None, 'tile'), may hold values from 0.2 to 0.4
- obs_value: float32 [16384, 128], P(('mem', 'tile')), may hold values from -6 to 6
- obs_weight: float32 [16384, 128], P(('mem', 'tile')), may hold values from 0.25 to 4
- obs_segment: int32 [16384], P(('mem', 'tile')), may hold values from 0 to 511
- obs_kind: int32 [16384], P(('mem', 'tile')), may hold values from 0 to 3
- obs_target: int32 [16384, 1], P(('mem', 'tile')), may hold values from 0 to 7; in each aligned block of 64 rows (0 to 63, 64 to 127, ...) at most 16 rows name the same one
- obs_count: int32 [256], P(('mem', 'tile')), may hold values from 1 to 64, 8192 in all
- operators: float32 [4, 128, 128], replicated, may hold values from -0.5 to 0.5
Outputs:
- increment: float32 [8, 128, 512], P(None, 'tile')
- gradient: float32 [32, 8, 128, 512], P('mem', None, 'tile')
The draws below stay inside these ranges and needn't reach their ends.
Inputs may be any that keep to these rules, and one draw needn't show every extreme that they name: `obs_target`: in the 64 rows of one owner no tile is named by more than 16 rows. The first obs_count slots of an owner hold observations, the others are empty and ignored.
All inputs are finite; a program needn't handle non-finite values. No bound on the sum of `obs_count` on one device may be relied on, other than what follows from the above.
Results may differ from the reference program's by a relative error of at most 0.0003.
Values sent between devices are 32-bit elements; how exact they have to be, the bound alone decides.
A program may use at most 64 MiB of HBM per device.

```python
import math
import jax
import jax.numpy as jnp
import numpy as np
from jax import lax

LEVELS = 8
LAT_DEV = 16
LON = 512
SEG = 128
OPS = 4
SLOTS = 64
SWEEPS = 16
MEMBERS = 32
LAT = 128
OWNED = 16384
CAP = 16
SEGS_TILE = 512
N_TILE = 8
DEVICES = 256


def draw_weights(key, part):
    split_keys = jax.random.split(key, 5)
    full_shape = (MEMBERS, LEVELS, LAT, LON)
    member_sign = (jax.random.randint(split_keys[0], (MEMBERS, 1, 1, 1), 0, 2) * 2 - 1).astype(jnp.float32)
    phase_lat = jax.random.uniform(split_keys[2], (MEMBERS, LEVELS, 1, 1), jnp.float32, 0.0, 2.0 * math.pi)
    phase_lon = jax.random.uniform(split_keys[4], (MEMBERS, LEVELS, 1, 1), jnp.float32, 0.0, 2.0 * math.pi)
    row_index = jnp.arange(LAT).astype(jnp.float32)[None, None, :, None]
    col_index = jnp.arange(LON).astype(jnp.float32)[None, None, None, :]
    ripple = jnp.sin(2.0 * math.pi * row_index / LAT + phase_lat) * jnp.cos(2.0 * math.pi * col_index / LON + phase_lon)
    amplitude = jax.random.uniform(split_keys[1], (MEMBERS, LEVELS, 1, 1), jnp.float32, 0.6, 1.2)
    roughness = jnp.clip(0.5 * jax.random.normal(split_keys[3], full_shape, jnp.float32), -1.4, 1.4)
    return member_sign * amplitude * (1.0 + 0.3 * ripple) + roughness


def set_ends(drawn, own_key, least, largest):
    shape = drawn.shape
    place = [jax.random.randint(jax.random.fold_in(own_key, axis), (), 0, shape[axis]) for axis in range(len(shape))]
    drawn = drawn.at[tuple(place)].set(least)
    longest = shape.index(max(shape))
    place[longest] = (place[longest] + 1) % shape[longest]
    return drawn.at[tuple(place)].set(largest)


def block_scale(rng, extent, cuts, low, top_value):
    loudness = 1.0
    for dim, blocks in cuts:
        draws = jax.random.uniform(jax.random.fold_in(jax.random.fold_in(rng, 6), dim), (blocks,), jnp.float32, low / len(cuts), top_value / len(cuts))
        loudness = loudness * jnp.repeat(jnp.exp(draws), extent[dim] // blocks).reshape((-1,) + (1,) * (len(extent) - 1 - dim))
    return loudness


def length_profile(count, total, limit, skew):
    portions = [(1 << 20) // math.isqrt(standing ** skew) + 1 for standing in range(2, count + 1)]
    spare, holding = total - limit - (count - 1), [1] * (count - 1)
    while spare > 0:
        candidates = [i for i in range(count - 1) if holding[i] < limit]
        pool, budget = sum([portions[i] for i in candidates]), spare
        for i in candidates:
            more = min(limit - holding[i], max(1, budget * portions[i] // pool), spare)
            holding[i] = holding[i] + more
            spare = spare - more
    return np.array([limit] + holding)


def ragged_sizes(stream_key, amount, total, limit, skew):
    if amount == 2:
        one = jax.random.randint(stream_key, (), max(1, total - limit), min(limit, total - 1) + 1)
        return jnp.stack([one, total - one])
    tallies = jnp.asarray(length_profile(amount, total, limit, skew), jnp.int32)
    twos = (amount - 1) // 2
    donor, sink = tallies[1:1 + 2 * twos:2], tallies[2:2 + 2 * twos:2]
    slack = jnp.minimum(donor - 1, limit - sink)
    passed = jax.random.randint(jax.random.fold_in(stream_key, 1), (twos,), 0, 1 << 20) % (slack + 1)
    tallies = tallies.at[1:1 + 2 * twos:2].set(donor - passed).at[2:2 + 2 * twos:2].set(sink + passed)
    return tallies[jax.random.permutation(jax.random.fold_in(stream_key, 2), amount)]


def shared_out(own_key, own, number, rows, number_of, top, most, slope):
    sequence = jax.random.permutation(own_key, number_of)
    heavy_load, ordinary = shares(number_of, rows * top, most, slope, True), shares(number_of, rows * top, most, slope, False)
    places = jnp.arange(number_of)

    def named(lengths, rotation):
        used = int((lengths > 0).sum())
        fixed = max(1, used // 4)
        moved = fixed + (places - fixed + rotation * (used - fixed)) % max(1, number_of - fixed)
        return jnp.zeros((number_of,), jnp.int32).at[sequence[jnp.where(places < fixed, places, moved)]].set(jnp.asarray(lengths, jnp.int32))

    lengths = jnp.where(number % 4 == 0, named(heavy_load, number // 4), named(ordinary, number - number // 4 - 1))
    mixed = jax.random.permutation(jax.random.fold_in(own, 3), number_of)
    giver, sink = mixed[0:number_of // 2 * 2:2], mixed[1:number_of // 2 * 2:2]
    margin = jnp.minimum(lengths[giver] - 1, most - lengths[sink]) // 2
    margin = jnp.where((giver == sequence[0]) | (sink == sequence[0]) | (lengths[sink] == 0), 0, jnp.maximum(margin, 0))
    moved = jax.random.randint(jax.random.fold_in(own, 4), (number_of // 2,), 0, 1 << 20) % (margin + 1)
    lengths = lengths.at[giver].add(-moved).at[sink].add(moved)
    items = jnp.searchsorted(jnp.cumsum(lengths), jnp.arange(rows * top), side="right").astype(jnp.int32)
    listing = items.reshape(top, rows).T
    listing = listing[jax.random.permutation(jax.random.fold_in(own, 1), rows)]
    rotation = jax.random.randint(jax.random.fold_in(own, 2), (rows, 1), 0, top)
    return jnp.take_along_axis(listing, (jnp.arange(top)[None, :] + rotation) % top, axis=1)


def shares(amount, total, limit, lean, full):
    loads = [(1 << 20) // math.isqrt(standing ** lean) + 1 for standing in range(1, amount + 1)]
    largest = limit if full else min(limit, max(-(-total // amount), total * loads[0] // sum(loads)))
    least = 1 if total - largest >= amount - 1 else 0
    counts, spare = [largest] + [least] * (amount - 1), total - largest - least * (amount - 1)
    while spare > 0:
        free = [i for i in range(1, amount) if counts[i] < largest] or [i for i in range(1, amount) if counts[i] < limit]
        pool, budget = sum([loads[i] for i in free]), spare
        for i in free:
            more = min(limit - counts[i], max(1, budget * loads[i] // pool), spare)
            counts[i] = counts[i] + more
            spare = spare - more
    return np.array(counts)


def bell_draw(rng, extent, width, bound, cuts=(), kind=jnp.bfloat16):
    values = width * jax.random.normal(rng, extent, jnp.float32)
    if cuts:
        values = values * block_scale(rng, extent, cuts, -0.22, 0.18)
    return jnp.clip(values, -bound, bound).astype(kind)


def setup_inputs(seed: int = 0) -> dict:
    seeds = jax.random.split(jax.random.key(seed), 12)
    weights = draw_weights(jax.random.fold_in(seeds[11], 71), 0)
    perturb = bell_draw(seeds[1], (MEMBERS, LEVELS, LAT, LON), 1.0, 6.0, ((0, 32), (2, 8)))
    coef_lon = jnp.clip(jnp.exp(math.log(0.09) - 2.1972246 * jax.random.uniform(seeds[2], (LEVELS, LAT, LON), jnp.float32) ** block_scale(seeds[2], (LEVELS, LAT, LON), ((1, 8),), -0.2, 0.2)), 0.01, 0.09)
    coef_lat = jnp.clip(jnp.exp(math.log(0.4) - 0.6931472 * jax.random.uniform(seeds[3], (LEVELS, LAT, LON), jnp.float32) ** block_scale(seeds[3], (LEVELS, LAT, LON), ((1, 8),), -0.2, 0.2)), 0.2, 0.4)
    obs_value = bell_draw(seeds[4], (OWNED, SEG), 1.0, 6.0, ((0, 256),), jnp.float32)
    obs_weight = jnp.clip(jnp.exp(math.log(4.0) - 2.7725887 * jax.random.uniform(seeds[5], (OWNED, SEG), jnp.float32) ** block_scale(seeds[5], (OWNED, SEG), ((0, 256),), -0.2, 0.2)), 0.25, 4.0)
    obs_segment = set_ends(jax.random.randint(seeds[6], (OWNED,), 0, SEGS_TILE), jax.random.fold_in(seeds[6], 1), 0, SEGS_TILE - 1).astype(jnp.int32)
    obs_kind = set_ends(jax.random.randint(seeds[7], (OWNED,), 0, OPS), jax.random.fold_in(seeds[7], 1), 0, OPS - 1).astype(jnp.int32)
    obs_target_keys = jax.random.split(jax.random.fold_in(seeds[8], 1), OWNED // SLOTS)
    obs_target_turns = jax.random.permutation(jax.random.fold_in(seeds[8], 3), OWNED // SLOTS)
    obs_target = jax.vmap(lambda own, number: shared_out(jax.random.fold_in(seeds[8], 2), own, number, SLOTS, N_TILE, 1, CAP, 2))(obs_target_keys, obs_target_turns).reshape((OWNED, 1))
    obs_count = ragged_sizes(seeds[9], DEVICES, DEVICES * SLOTS // 2, SLOTS, 2).astype(jnp.int32)
    operators = bell_draw(seeds[10], (OPS, SEG, SEG), SEG ** -0.5, 0.5, (), jnp.float32)
    return dict(weights=weights, perturb=perturb, coef_lon=coef_lon, coef_lat=coef_lat, obs_value=obs_value, obs_weight=obs_weight, obs_segment=obs_segment, obs_kind=obs_kind, obs_target=obs_target, obs_count=obs_count, operators=operators)


def zero_rows(current):
    return jnp.pad(current, ((0, 0), (1, 1), (0, 0)))

def advance(current, padded, coef_lon, coef_lat):
    zonal_term = jnp.roll(current, 1, 2) + jnp.roll(current, -1, 2) - 2.0 * current
    across = padded[:, 2:] + padded[:, :-2] - 2.0 * current
    return current + coef_lon * zonal_term + coef_lat * across

def retreat(current, padded_lat, coef_lon, coef_lat):
    flux_lon = coef_lon * current
    retain = 1.0 - 2.0 * coef_lon - 2.0 * coef_lat
    return retain * current + jnp.roll(flux_lon, 1, 2) + jnp.roll(flux_lon, -1, 2) + padded_lat[:, 2:] + padded_lat[:, :-2]

def smooth_forward(current, coef_lon, coef_lat):
    for sweep_index in range(SWEEPS):
        current = advance(current, zero_rows(current), coef_lon, coef_lat)
    return current

def smooth_adjoint(current, coef_lon, coef_lat):
    for sweep_index in range(SWEEPS):
        current = retreat(current, zero_rows(coef_lat * current), coef_lon, coef_lat)
    return current

def observe(blocks, operators, kinds, values, precisions):
    images = jnp.einsum('bj,kij->kbi', blocks, operators, precision=lax.Precision.HIGHEST)
    choose = (kinds[None, :] == jnp.arange(operators.shape[0]).astype(jnp.int32)[:, None]).astype(jnp.float32)[:, :, None]
    modelled = lax.optimization_barrier(jnp.sum(choose * images, 0))
    misfit = precisions * (modelled - values)
    return jnp.einsum('kbi,kij->bj', choose * misfit[None], operators, precision=lax.Precision.HIGHEST)

def reference(weights, perturb, coef_lon, coef_lat, obs_value, obs_weight, obs_segment, obs_kind, obs_target, obs_count, operators):
    scale = 1.0 / math.sqrt(MEMBERS)

    def add_member(member, accum):
        smoothed = smooth_forward(weights[member], coef_lon, coef_lat)
        return accum + perturb[member].astype(jnp.float32) * smoothed
    summed = lax.fori_loop(0, MEMBERS, add_member, jnp.zeros((LEVELS, LAT, LON), jnp.float32))
    increment = summed * scale
    segs_tile = LEVELS * LAT_DEV * LON // SEG
    table = increment.reshape(LEVELS, N_TILE, LAT_DEV, LON).transpose(1, 0, 2, 3).reshape(N_TILE * segs_tile, SEG)
    positions = jnp.arange(OWNED).astype(jnp.int32)
    owner = positions // SLOTS
    live = (positions % SLOTS < obs_count[owner]).astype(jnp.float32)
    global_id = (obs_target[:, 0] * segs_tile + obs_segment).astype(jnp.int32)
    adjoint = observe(table[global_id], operators, obs_kind, obs_value, obs_weight * live[:, None])
    deposited = jnp.zeros_like(table).at[global_id].add(adjoint)
    adjoint_field = deposited.reshape(N_TILE, LEVELS, LAT_DEV, LON).transpose(1, 0, 2, 3).reshape(LEVELS, LAT, LON)

    def member_gradient(pair):
        return pair[0] + smooth_adjoint(pair[1].astype(jnp.float32) * adjoint_field, coef_lon, coef_lat) * scale
    gradient = lax.map(member_gradient, (weights, perturb))
    return (increment, gradient)
```

```python
import math

import jax
import jax.numpy as jnp
from jax import lax
from jax.experimental import pallas as pl
from jax.experimental.pallas import tpu as pltpu
from jax.sharding import PartitionSpec as P

SWEEPS = 16
MEM = 32
TILES = 8
MESH = pl.DeviceIdType.MESH
HIGHEST = lax.Precision.HIGHEST
F32 = jnp.float32


def eye_mask(n):
    return lax.broadcasted_iota(jnp.int32, (n, n), 0) == lax.broadcasted_iota(jnp.int32, (n, n), 1)


def column(row):
    return jnp.sum(jnp.where(eye_mask(row.shape[1]), row, 0.0), axis=1, keepdims=True)


def as_row(col):
    return jnp.sum(jnp.where(eye_mask(col.shape[0]), col, 0.0), axis=0, keepdims=True)


def chunk_of(member, tile):
    return lax.rem(member // 4 + tile, TILES), lax.rem(member, 4)


def kernel(
    w_ref, p_ref, clon_ref, clat_ref, ov_ref, ow_ref, seg_ref, kind_ref, tgt_ref, cnt_ref, op_ref,
    inc_ref, back_ref,
    wbuf, lonbuf, latbuf, pbuf, pf, pin, north, south, retain,
    field, pack, packin, rs1, rs2, red1, red2, adj, fld, gbuf,
    in_send, in_recv, loc_sem, obs_send, obs_recv, out_send, out_recv,
    rs_send, rs_recv, ag_send, ag_recv, ag_own,
):
    m = lax.axis_index("mem")
    t = lax.axis_index("tile")
    scale = 1.0 / math.sqrt(MEM)

    load_p = pltpu.make_async_copy(p_ref.at[0], pin, loc_sem.at[0])
    load_p.start()
    own = [
        pltpu.make_async_copy(w_ref.at[0, t], wbuf.at[t], loc_sem.at[1]),
        pltpu.make_async_copy(clon_ref.at[t], lonbuf.at[t], loc_sem.at[2]),
        pltpu.make_async_copy(clat_ref.at[t], latbuf.at[t], loc_sem.at[3]),
    ]
    for copy in own:
        copy.start()

    barrier = pltpu.get_barrier_semaphore()
    for d in range(1, TILES):
        pl.semaphore_signal(
            barrier, inc=1, device_id=(m, lax.rem(t + d, TILES)), device_id_type=MESH
        )

    def greet(d, carry):
        pl.semaphore_signal(
            barrier, inc=1, device_id=(lax.rem(m + d, MEM), t), device_id_type=MESH
        )
        return carry

    lax.fori_loop(1, MEM, greet, 0)
    pl.semaphore_wait(barrier, TILES - 1 + MEM - 1)

    sends = []
    for a, (src, dst) in enumerate(((w_ref.at[0], wbuf), (clon_ref, lonbuf), (clat_ref, latbuf))):
        for d in range(1, TILES):
            peer = lax.rem(t + d, TILES)
            copy = pltpu.make_async_remote_copy(
                src_ref=src.at[peer], dst_ref=dst.at[t],
                send_sem=in_send.at[a, d], recv_sem=in_recv.at[a, d],
                device_id=(m, peer), device_id_type=MESH,
            )
            copy.start()
            sends.append(copy)

    load_p.wait()
    pf[...] = pin[...].astype(F32)
    psends = []
    for d in range(1, TILES):
        peer = lax.rem(t + d, TILES)
        copy = pltpu.make_async_remote_copy(
            src_ref=pf.at[peer], dst_ref=pbuf.at[t],
            send_sem=in_send.at[3, d], recv_sem=in_recv.at[3, d],
            device_id=(m, peer), device_id_type=MESH,
        )
        copy.start()
        psends.append(copy)
    own_p = pltpu.make_async_copy(pf.at[t], pbuf.at[t], loc_sem.at[4])
    own_p.start()

    slots = ov_ref.shape[0]
    live = lax.broadcasted_iota(jnp.int32, (slots, 1), 0) < cnt_ref[0]
    lane = lax.broadcasted_iota(jnp.int32, (slots, 128), 1)
    target = as_row(tgt_ref[...].astype(F32))
    seg_col = column(seg_ref[...].astype(F32))
    kind_col = column(kind_ref[...].astype(F32))
    named = (
        target == lax.broadcasted_iota(jnp.int32, (TILES, slots), 0).astype(F32)
    ).astype(F32)
    upper = (
        lax.broadcasted_iota(jnp.int32, (slots, slots), 0)
        < lax.broadcasted_iota(jnp.int32, (slots, slots), 1)
    ).astype(F32)
    earlier = jnp.dot(named, upper, preferred_element_type=F32)
    place = target * 16.0 + jnp.sum(earlier * named, axis=0, keepdims=True)
    route = (
        lax.broadcasted_iota(jnp.int32, (128, slots), 0).astype(F32) == place
    ).astype(F32)
    precision = jnp.where(live, ow_ref[...], 0.0)
    meta = jnp.where(lane == 0, seg_col, jnp.where(lane == 1, kind_col, 0.0))
    rows = jnp.concatenate([ov_ref[...], precision, meta], axis=1)
    routed = jnp.dot(route, rows, precision=HIGHEST, preferred_element_type=F32)
    pack[:, 0:16, :] = routed[:, 0:128].reshape(TILES, 16, 128)
    pack[:, 16:32, :] = routed[:, 128:256].reshape(TILES, 16, 128)
    routed_meta = routed[:, 256:384].reshape(TILES, 16, 128)
    pack[:, 32:40, :] = routed_meta[:, 0:8] + pltpu.roll(routed_meta[:, 8:16], 64, 2)
    osends = []
    for d in range(1, TILES):
        peer = lax.rem(t + d, TILES)
        copy = pltpu.make_async_remote_copy(
            src_ref=pack.at[peer], dst_ref=packin.at[t],
            send_sem=obs_send.at[d], recv_sem=obs_recv.at[d],
            device_id=(m, peer), device_id_type=MESH,
        )
        copy.start()
        osends.append(copy)
    own_o = pltpu.make_async_copy(pack.at[t], packin.at[t], loc_sem.at[5])
    own_o.start()

    for copy in own:
        copy.wait()
    for copy in sends:
        copy.wait_recv()

    row_index = lax.broadcasted_iota(jnp.int32, (128, 512), 0)
    lon = lonbuf[...].reshape(128, 512)
    lat = latbuf[...].reshape(128, 512)
    retain[...] = 1.0 - 2.0 * lon - 2.0 * lat
    north[...] = jnp.where(row_index == 0, 0.0, lat)
    south[...] = jnp.where(row_index == 127, 0.0, lat)
    field[...] = wbuf[...].reshape(128, 512)

    def sweep(step, carry):
        a = field[...]
        zonal = pltpu.roll(a, 1, 1) + pltpu.roll(a, 511, 1)
        field[...] = (
            retain[...] * a
            + lonbuf[...].reshape(128, 512) * zonal
            + north[...] * pltpu.roll(a, 1, 0)
            + south[...] * pltpu.roll(a, 127, 0)
        )
        return carry

    lax.fori_loop(0, SWEEPS, sweep, 0)
    own_p.wait()
    for copy in psends:
        copy.wait_recv()
    gbuf[...] = field[...].reshape(TILES, 16, 512) * pbuf[...]

    def add_up(index, src, rs, red, dst):
        lead, quarter = chunk_of(m, t)
        cols = pl.ds(pl.multiple_of(quarter * 128, 128), 128)

        def scatter(d, carry):
            peer = lax.rem(m + d, MEM)
            plead, pquarter = chunk_of(peer, t)
            pcols = pl.ds(pl.multiple_of(pquarter * 128, 128), 128)
            pltpu.make_async_remote_copy(
                src_ref=src.at[plead, :, pcols], dst_ref=rs.at[m],
                send_sem=rs_send.at[index], recv_sem=rs_recv.at[index],
                device_id=(peer, t), device_id_type=MESH,
            ).start()
            return carry

        lax.fori_loop(1, MEM, scatter, 0)
        rs[m] = src[lead, :, cols]
        got = rs.at[pl.ds(0, MEM - 1)]
        pltpu.make_async_copy(got, got, rs_recv.at[index]).wait()
        red[...] = jnp.sum(rs[...], axis=0)

        def spread(d, carry):
            peer = lax.rem(m + d, MEM)
            pltpu.make_async_remote_copy(
                src_ref=red, dst_ref=dst.at[t, :, cols],
                send_sem=ag_send.at[index], recv_sem=ag_recv.at[index],
                device_id=(peer, lead), device_id_type=MESH,
            ).start()
            return carry

        lax.fori_loop(1, MEM, spread, 0)

        @pl.when(lead == t)
        def _():
            pltpu.make_async_copy(red, dst.at[t, :, cols], ag_recv.at[index]).start()

        far = pltpu.make_async_remote_copy(
            src_ref=red, dst_ref=dst.at[t, :, cols],
            send_sem=ag_own.at[index], recv_sem=ag_recv.at[index],
            device_id=(m, lead), device_id_type=MESH,
        )

        @pl.when(lead != t)
        def _():
            far.start()

        pltpu.make_async_copy(dst, dst, ag_recv.at[index]).wait()
        sent = rs.at[pl.ds(0, MEM - 1)]
        pltpu.make_async_copy(sent, sent, rs_send.at[index]).wait()
        pltpu.make_async_copy(sent, sent, ag_send.at[index]).wait()

        @pl.when(lead != t)
        def _():
            far.wait_send()

    add_up(0, gbuf, rs1, red1, inc_ref)

    own_o.wait()
    for copy in osends:
        copy.wait_recv()
    value = packin[:, 0:16, :].reshape(128, 128)
    weight = packin[:, 16:32, :].reshape(128, 128)
    got = packin[:, 32:40, :]
    info = jnp.concatenate([got, pltpu.roll(got, 64, 2)], axis=1).reshape(128, 128)
    seg = info[:, 0:1]
    kind = info[:, 1:2]
    seg_row = as_row(seg)
    cell_row = lax.broadcasted_iota(jnp.int32, (128, 128), 1).astype(F32) * 4.0
    cell_col = lax.broadcasted_iota(jnp.int32, (128, 128), 0).astype(F32) * 4.0
    table = inc_ref[...]
    x = jnp.zeros((128, 128), F32)
    for q in range(4):
        pick = (seg == cell_row + float(q)).astype(F32)
        x = x + jnp.dot(
            pick, table[:, :, q * 128:(q + 1) * 128].reshape(128, 128),
            precision=HIGHEST, preferred_element_type=F32,
        )
    x = x * scale
    kinds = op_ref.shape[0]
    flat = jnp.concatenate([op_ref[k] for k in range(kinds)], axis=1)
    wide = jnp.concatenate([jnp.where(kind == float(k), x, 0.0) for k in range(kinds)], axis=1)
    modelled = lax.dot_general(
        wide, flat, (((1,), (1,)), ((), ())), precision=HIGHEST, preferred_element_type=F32
    )
    misfit = weight * (modelled - value)
    wide = jnp.concatenate([jnp.where(kind == float(k), misfit, 0.0) for k in range(kinds)], axis=1)
    z = jnp.dot(
        wide, op_ref[...].reshape(kinds * 128, 128), precision=HIGHEST, preferred_element_type=F32
    )
    for q in range(4):
        put = (seg_row == cell_col + float(q)).astype(F32)
        adj[:, :, q * 128:(q + 1) * 128] = jnp.dot(
            put, z, precision=HIGHEST, preferred_element_type=F32
        ).reshape(TILES, 16, 128)

    add_up(1, adj, rs2, red2, fld)

    field[...] = (fld[...] * pbuf[...]).reshape(128, 512)

    def sweep_back(step, carry):
        g = field[...]
        flux = lonbuf[...].reshape(128, 512) * g
        field[...] = (
            retain[...] * g
            + pltpu.roll(flux, 1, 1) + pltpu.roll(flux, 511, 1)
            + pltpu.roll(north[...] * g, 127, 0)
            + pltpu.roll(south[...] * g, 1, 0)
        )
        return carry

    lax.fori_loop(0, SWEEPS, sweep_back, 0)
    gback = wbuf
    for copy in sends:
        copy.wait_send()
    gback[...] = field[...].reshape(TILES, 16, 512)
    bsends = []
    for d in range(1, TILES):
        peer = lax.rem(t + d, TILES)
        copy = pltpu.make_async_remote_copy(
            src_ref=gback.at[peer], dst_ref=back_ref.at[t],
            send_sem=out_send.at[d], recv_sem=out_recv.at[d],
            device_id=(m, peer), device_id_type=MESH,
        )
        copy.start()
        bsends.append(copy)
    own_b = pltpu.make_async_copy(gback.at[t], back_ref.at[t], loc_sem.at[6])
    own_b.start()
    for copy in psends + osends:
        copy.wait_send()
    own_b.wait()
    for copy in bsends:
        copy.wait()


def shards(
    weights, perturb, coef_lon, coef_lat, obs_value, obs_weight,
    obs_segment, obs_kind, obs_target, obs_count, operators,
):
    scale = 1.0 / math.sqrt(MEM)
    vmem = pl.BlockSpec(memory_space=pltpu.VMEM)
    hbm = pl.BlockSpec(memory_space=pl.ANY)
    smem = pl.BlockSpec(memory_space=pltpu.SMEM)
    block = (TILES, 16, 512)
    flat = (128, 512)
    dma = pltpu.SemaphoreType.DMA
    inc, back = pl.pallas_call(
        kernel,
        out_shape=(jax.ShapeDtypeStruct(block, F32), jax.ShapeDtypeStruct(block, F32)),
        in_specs=[hbm, hbm, hbm, hbm, vmem, vmem, vmem, vmem, vmem, smem, vmem],
        out_specs=(vmem, vmem),
        scratch_shapes=[
            pltpu.VMEM(block, F32), pltpu.VMEM(block, F32), pltpu.VMEM(block, F32),
            pltpu.VMEM(block, F32), pltpu.VMEM(block, F32), pltpu.VMEM(block, jnp.bfloat16),
            pltpu.VMEM(flat, F32), pltpu.VMEM(flat, F32), pltpu.VMEM(flat, F32),
            pltpu.VMEM(flat, F32),
            pltpu.VMEM((TILES, 40, 128), F32), pltpu.VMEM((TILES, 40, 128), F32),
            pltpu.VMEM((MEM, 16, 128), F32), pltpu.VMEM((MEM, 16, 128), F32),
            pltpu.VMEM((16, 128), F32), pltpu.VMEM((16, 128), F32),
            pltpu.VMEM(block, F32), pltpu.VMEM(block, F32), pltpu.VMEM(block, F32),
            dma((4, TILES)), dma((4, TILES)), dma((7,)), dma((TILES,)), dma((TILES,)),
            dma((TILES,)), dma((TILES,)),
            dma((2,)), dma((2,)), dma((2,)), dma((2,)), dma((2,)),
        ],
        compiler_params=pltpu.CompilerParams(collective_id=0, has_side_effects=True),
    )(
        weights, perturb, coef_lon, coef_lat, obs_value, obs_weight,
        obs_segment.reshape(1, -1), obs_kind.reshape(1, -1), obs_target, obs_count, operators,
    )
    return inc * scale, weights + (back * scale)[None]


def solution(mesh):
    placed = (
        P("mem", None, "tile", None),
        P("mem", None, "tile", None),
        P(None, "tile", None),
        P(None, "tile", None),
        P(("mem", "tile"), None),
        P(("mem", "tile"), None),
        P(("mem", "tile")),
        P(("mem", "tile")),
        P(("mem", "tile"), None),
        P(("mem", "tile")),
        P(),
    )
    return jax.shard_map(
        shards,
        mesh=mesh,
        in_specs=placed,
        out_specs=(P(None, "tile", None), P("mem", None, "tile", None)),
        check_vma=False,
    )
```

```python
import math

import jax
import jax.numpy as jnp
from jax import lax
from jax.experimental import pallas as pl
from jax.experimental.pallas import tpu as pltpu
from jax.sharding import PartitionSpec as P

SWEEPS = 16
MEM = 32
TILES = 8
MESH = pl.DeviceIdType.MESH
HIGHEST = lax.Precision.HIGHEST
F32 = jnp.float32
BF16 = jnp.bfloat16


def eye_mask(n):
    return lax.broadcasted_iota(jnp.int32, (n, n), 0) == lax.broadcasted_iota(jnp.int32, (n, n), 1)


def column(row):
    return jnp.sum(jnp.where(eye_mask(row.shape[1]), row, 0.0), axis=1, keepdims=True)


def as_row(col):
    return jnp.sum(jnp.where(eye_mask(col.shape[0]), col, 0.0), axis=0, keepdims=True)


def split3(x):
    hi = x.astype(BF16)
    rest = x - hi.astype(F32)
    mid = rest.astype(BF16)
    low = (rest - mid.astype(F32)).astype(BF16)
    return jnp.concatenate([hi, mid, low], axis=1)


def select(onehot, parts):
    width = parts.shape[1] // 3
    got = jnp.dot(onehot.astype(BF16), parts, preferred_element_type=F32)
    return got[:, 0:width] + got[:, width:2 * width] + got[:, 2 * width:3 * width]


def aligned(index, size):
    return pl.ds(pl.multiple_of(index * size, size), size)


def kernel(
    w_ref, p_ref, clon_ref, clat_ref, ov_ref, ow_ref, seg_ref, kind_ref, tgt_ref, cnt_ref, op_ref,
    inc_ref, back_ref,
    wbuf, coef, pbuf, pf, pin, north, south, retain, field,
    pack, lists, ad, ybuf, s2, zbuf, prod, sibp, half, rs, inc_red, adj_red, fld,
    loc_sem, snd, rcv,
):
    m = lax.axis_index("mem")
    t = lax.axis_index("tile")
    y = m // 8
    z = lax.rem(m // 2, 4)
    c = lax.rem(m, 2)
    sib = m + 1 - 2 * c
    place16 = m // 2
    scale = 1.0 / math.sqrt(MEM)
    lead = lax.rem(2 * y + z // 2 + t, TILES)
    cols = aligned(2 * c + lax.rem(z, 2), 128)

    def remote(src, dst, sem, member, tile):
        return pltpu.make_async_remote_copy(
            src_ref=src, dst_ref=dst, send_sem=snd.at[sem], recv_sem=rcv.at[sem],
            device_id=(member, tile), device_id_type=MESH,
        )

    def got(ref, sem):
        pltpu.make_async_copy(ref, ref, rcv.at[sem]).wait()

    def left(ref, sem):
        pltpu.make_async_copy(ref, ref, snd.at[sem]).wait()

    def greet(member, tile):
        pl.semaphore_signal(
            pltpu.get_barrier_semaphore(), inc=1, device_id=(member, tile), device_id_type=MESH
        )

    load_p = pltpu.make_async_copy(p_ref.at[0], pin, loc_sem.at[0])
    load_p.start()
    piece = (aligned(c, 8), aligned(y, 128))
    own = [
        pltpu.make_async_copy(w_ref.at[0, t], wbuf.at[t], loc_sem.at[1]),
        pltpu.make_async_copy(clon_ref.at[(t,) + piece], coef.at[(0, t) + piece], loc_sem.at[2]),
        pltpu.make_async_copy(clat_ref.at[(t,) + piece], coef.at[(1, t) + piece], loc_sem.at[3]),
    ]
    for copy in own:
        copy.start()

    for d in range(1, TILES):
        greet(m, lax.rem(t + d, TILES))
    greet(sib, t)

    def greet_core(d, carry):
        greet(2 * lax.rem(place16 + d, 16) + c, t)
        return carry

    lax.fori_loop(1, 16, greet_core, 0)
    for source in range(4):
        tile = lax.rem(t + 2 * y + z // 2, TILES)

        @pl.when((tile != t) | (z != source))
        def _(source=source, tile=tile):
            greet(y * 8 + source * 2 + c, tile)

    slots = ov_ref.shape[0]
    live = lax.broadcasted_iota(jnp.int32, (slots, 1), 0) < cnt_ref[0]
    lane = lax.broadcasted_iota(jnp.int32, (slots, 128), 1)
    target = tgt_ref[...].astype(F32)
    seg_col = column(seg_ref[...].astype(F32))
    kind_col = column(kind_ref[...].astype(F32))
    named = (
        target == lax.broadcasted_iota(jnp.int32, (TILES, slots), 0).astype(F32)
    ).astype(F32)
    upper = (
        lax.broadcasted_iota(jnp.int32, (slots, slots), 0)
        < lax.broadcasted_iota(jnp.int32, (slots, slots), 1)
    ).astype(F32)
    earlier = jnp.dot(named, upper, preferred_element_type=F32)
    place = target * 16.0 + jnp.sum(earlier * named, axis=0, keepdims=True)
    route = (
        lax.broadcasted_iota(jnp.int32, (128, slots), 0).astype(F32) == place
    ).astype(F32)
    precision = jnp.where(live, ow_ref[...], 0.0)
    meta = jnp.where(lane == 0, seg_col, jnp.where(lane == 1, kind_col, 0.0))
    routed = select(route, split3(jnp.concatenate([ov_ref[...], precision, meta], axis=1)))
    pack[:, 0:16, :] = routed[:, 0:128].reshape(TILES, 16, 128)
    pack[:, 16:32, :] = routed[:, 128:256].reshape(TILES, 16, 128)
    routed_meta = routed[:, 256:384].reshape(TILES, 16, 128)
    pack[:, 32:40, :] = routed_meta[:, 0:8] + pltpu.roll(routed_meta[:, 8:16], 64, 2)
    load_p.wait()
    pf[...] = pin[...].astype(F32)

    away = jnp.where((y == 0) & (z < 2), 3, 4)
    pl.semaphore_wait(pltpu.get_barrier_semaphore(), TILES - 1 + 1 + 15 + away)

    for d in range(1, TILES):
        peer = lax.rem(t + d, TILES)
        remote(clon_ref.at[(peer,) + piece], coef.at[(0, t) + piece], 0, m, peer).start()
        remote(clat_ref.at[(peer,) + piece], coef.at[(1, t) + piece], 0, m, peer).start()
    for d in range(1, TILES):
        peer = lax.rem(t + d, TILES)
        remote(pack.at[peer], lists.at[c, t], 1, m, peer).start()
    own_o = pltpu.make_async_copy(pack.at[t], lists.at[c, t], loc_sem.at[5])
    own_o.start()
    for d in range(1, TILES):
        peer = lax.rem(t + d, TILES)
        remote(w_ref.at[0, peer], wbuf.at[t], 2, m, peer).start()
    for d in range(1, TILES):
        peer = lax.rem(t + d, TILES)
        remote(pf.at[peer], pbuf.at[t], 3, m, peer).start()
    own_p = pltpu.make_async_copy(pf.at[t], pbuf.at[t], loc_sem.at[4])
    own_p.start()

    own[1].wait()
    own[2].wait()
    got(rs.at[pl.ds(0, 7)], 0)
    part = coef.at[(slice(None), slice(None)) + piece]
    for d in range(1, 4):
        remote(part, part, 4, lax.rem(y + d, 4) * 8 + z * 2 + c, t).start()

    own_o.wait()
    got(pack.at[pl.ds(0, 7)], 1)
    remote(lists.at[c], lists.at[c], 5, sib, t).start()

    got(wbuf.at[pl.ds(0, 6)], 4)
    rows8 = coef.at[:, :, piece[0], :]
    remote(rows8, rows8, 6, sib, t).start()

    got(lists.at[0], 5)

    rows = lists[...].reshape(2 * TILES, 40, 128)
    value = rows[:, 0:16].reshape(256, 128)
    weight = rows[:, 16:32].reshape(256, 128)
    info = rows[:, 32:40]
    info = jnp.concatenate([info, pltpu.roll(info, 64, 2)], axis=1).reshape(256, 128)
    kind = info[:, 1:2]
    key = as_row(info[:, 0:1] + 512.0 * kind)
    kinds = op_ref.shape[0]
    flat = op_ref[...].reshape(kinds * 128, 128)
    weighted = weight * value
    wide = jnp.concatenate([jnp.where(kind == float(k), weighted, 0.0) for k in range(kinds)], axis=1)
    pulled = jnp.dot(wide, flat, precision=HIGHEST, preferred_element_type=F32)
    weight_parts = split3(weight)
    pulled_parts = split3(pulled)
    cell = lax.broadcasted_iota(jnp.int32, (128, 256), 0)
    level = lax.rem(t - cell // 16 + TILES, TILES)
    cell = (level * 64 + lax.rem(cell, 16) * 4 + 2 * c).astype(F32)
    for b in range(2):
        every = jnp.zeros((128, 256), F32)
        span = pl.ds(b * 128, 128)
        for k in range(kinds):
            onehot = (key == cell + float(b + 512 * k)).astype(F32)
            every = every + onehot
            ad[k, :, :, span] = select(onehot, weight_parts).reshape(TILES, 16, 128)
        ad[kinds, :, :, span] = select(every, pulled_parts).reshape(TILES, 16, 128)
    for d in range(1, 4):
        there = lax.rem(y + d, 4)
        remote(
            ad.at[:, pl.ds(2 * there, 2)], ybuf.at[y], 7, there * 8 + z * 2 + c, t
        ).start()

    got(rows8, 6)
    row_index = lax.broadcasted_iota(jnp.int32, (128, 512), 0)
    lon = coef[0].reshape(128, 512)
    lat = coef[1].reshape(128, 512)
    retain[...] = 1.0 - 2.0 * lon - 2.0 * lat
    north[...] = jnp.where(row_index == 0, 0.0, lat)
    south[...] = jnp.where(row_index == 127, 0.0, lat)

    own[0].wait()
    got(wbuf.at[pl.ds(0, 7)], 2)
    field[...] = wbuf[...].reshape(128, 512)

    def sweep(step, carry):
        a = field[...]
        zonal = pltpu.roll(a, 1, 1) + pltpu.roll(a, 511, 1)
        field[...] = (
            retain[...] * a
            + coef[0].reshape(128, 512) * zonal
            + north[...] * pltpu.roll(a, 1, 0)
            + south[...] * pltpu.roll(a, 127, 0)
        )
        return carry

    lax.fori_loop(0, SWEEPS, sweep, 0)
    own_p.wait()
    got(pbuf.at[pl.ds(0, 7)], 3)
    prod[...] = field[...].reshape(TILES, 16, 512) * pbuf[...]
    mine = aligned(c, 256)
    remote(prod.at[:, :, aligned(1 - c, 256)], sibp, 8, sib, t).start()

    got(sibp, 8)
    half[...] = prod[:, :, mine] + sibp[...]

    def scatter(d, carry):
        there = lax.rem(place16 + d, 16)
        ty = there // 4
        tz = lax.rem(there, 4)
        tlead = lax.rem(2 * ty + tz // 2 + t, TILES)
        remote(
            half.at[tlead, :, aligned(lax.rem(tz, 2), 128)], rs.at[place16], 9, 2 * there + c, t
        ).start()
        return carry

    lax.fori_loop(1, 16, scatter, 0)
    rs[place16] = half[lead, :, aligned(lax.rem(z, 2), 128)]

    got(ybuf.at[pl.ds(0, 3)], 7)
    ybuf[y] = ad[:, pl.ds(2 * y, 2)]
    s2[...] = ybuf[0] + ybuf[1] + ybuf[2] + ybuf[3]
    for tz in range(4):
        level_to = lax.rem(t - 2 * y - tz // 2 + TILES, TILES)
        block = s2.at[:, tz // 2, :, pl.ds((tz % 2) * 128, 128)]
        self = (level_to == t) & (z == tz)

        @pl.when(self)
        def _(block=block):
            pltpu.make_async_copy(block, zbuf.at[z], rcv.at[10]).start()

        @pl.when(jnp.logical_not(self))
        def _(block=block, tz=tz, level_to=level_to):
            remote(block, zbuf.at[z], 10, y * 8 + tz * 2 + c, level_to).start()

    got(rs.at[pl.ds(0, 15)], 9)
    total = jnp.sum(rs[...], axis=0)
    inc_red[...] = total

    got(zbuf, 10)
    normal = zbuf[0] + zbuf[1] + zbuf[2] + zbuf[3]
    images = lax.dot_general(
        total * scale, flat, (((1,), (1,)), ((), ())), precision=HIGHEST, preferred_element_type=F32
    )
    images = images * jnp.concatenate([normal[k] for k in range(kinds)], axis=1)
    adjoint = jnp.dot(images, flat, precision=HIGHEST, preferred_element_type=F32) - normal[kinds]
    adj_red[...] = adjoint


    def spread(d, carry):
        there = lax.rem(place16 + d, 16)
        remote(adj_red, fld.at[lead, :, cols], 11, 2 * there + c, t).start()
        return carry

    lax.fori_loop(1, 16, spread, 0)
    fld[lead, :, cols] = adjoint
    got(rs.at[pl.ds(0, 15)], 11)
    side = fld.at[:, :, mine]
    remote(side, side, 12, sib, t).start()

    def tell(d, carry):
        there = lax.rem(place16 + d, 16)
        remote(inc_red, inc_ref.at[t, :, cols], 13, 2 * there + c, lead).start()
        return carry

    lax.fori_loop(1, 16, tell, 0)
    far = remote(inc_red, inc_ref.at[t, :, cols], 14, m, lead)

    @pl.when(lead == t)
    def _():
        pltpu.make_async_copy(inc_red, inc_ref.at[t, :, cols], rcv.at[14]).start()

    @pl.when(lead != t)
    def _():
        far.start()

    got(side, 12)

    field[...] = (fld[...] * pbuf[...]).reshape(128, 512)

    def sweep_back(step, carry):
        g = field[...]
        flux = coef[0].reshape(128, 512) * g
        field[...] = (
            retain[...] * g
            + pltpu.roll(flux, 1, 1) + pltpu.roll(flux, 511, 1)
            + pltpu.roll(north[...] * g, 127, 0)
            + pltpu.roll(south[...] * g, 1, 0)
        )
        return carry

    lax.fori_loop(0, SWEEPS, sweep_back, 0)
    prod_free = half
    left(prod_free, 8)
    prod[...] = field[...].reshape(TILES, 16, 512)
    for d in range(1, TILES):
        peer = lax.rem(t + d, TILES)
        remote(prod.at[peer], back_ref.at[t], 15, m, peer).start()
    own_b = pltpu.make_async_copy(prod.at[t], back_ref.at[t], loc_sem.at[6])
    own_b.start()

    got(rs.at[pl.ds(0, 15)], 13)
    got(inc_red, 14)
    side_inc = inc_ref.at[:, :, mine]
    remote(side_inc, side_inc, 16, sib, t).start()

    own_b.wait()
    got(prod.at[pl.ds(0, 7)], 15)
    got(side_inc, 16)
    left(rs.at[pl.ds(0, 7)], 0)
    left(pack.at[pl.ds(0, 7)], 1)
    left(wbuf.at[pl.ds(0, 7)], 2)
    left(pf.at[pl.ds(0, 7)], 3)
    left(wbuf.at[pl.ds(0, 6)], 4)
    left(lists.at[0], 5)
    left(rows8, 6)
    left(ybuf.at[pl.ds(0, 3)], 7)
    left(rs.at[pl.ds(0, 15)], 9)

    @pl.when((y == 0) & (z < 2))
    def _():
        left(zbuf.at[pl.ds(0, 3)], 10)

    @pl.when((y > 0) | (z >= 2))
    def _():
        left(zbuf, 10)

    left(rs.at[pl.ds(0, 15)], 11)
    left(side, 12)
    left(rs.at[pl.ds(0, 15)], 13)

    @pl.when(lead != t)
    def _():
        far.wait_send()

    left(prod.at[pl.ds(0, 7)], 15)
    left(side_inc, 16)


def shards(
    weights, perturb, coef_lon, coef_lat, obs_value, obs_weight,
    obs_segment, obs_kind, obs_target, obs_count, operators,
):
    scale = 1.0 / math.sqrt(MEM)
    vmem = pl.BlockSpec(memory_space=pltpu.VMEM)
    hbm = pl.BlockSpec(memory_space=pl.ANY)
    smem = pl.BlockSpec(memory_space=pltpu.SMEM)
    block = (TILES, 16, 512)
    flat = (128, 512)
    dma = pltpu.SemaphoreType.DMA
    inc, back = pl.pallas_call(
        kernel,
        out_shape=(jax.ShapeDtypeStruct(block, F32), jax.ShapeDtypeStruct(block, F32)),
        in_specs=[hbm, hbm, hbm, hbm, vmem, vmem, vmem, vmem, vmem, smem, vmem],
        out_specs=(vmem, vmem),
        scratch_shapes=[
            pltpu.VMEM(block, F32), pltpu.VMEM((2,) + block, F32),
            pltpu.VMEM(block, F32), pltpu.VMEM(block, F32), pltpu.VMEM(block, BF16),
            pltpu.VMEM(flat, F32), pltpu.VMEM(flat, F32), pltpu.VMEM(flat, F32),
            pltpu.VMEM(flat, F32),
            pltpu.VMEM((TILES, 40, 128), F32), pltpu.VMEM((2, TILES, 40, 128), F32),
            pltpu.VMEM((5, 8, 16, 256), F32), pltpu.VMEM((4, 5, 2, 16, 256), F32),
            pltpu.VMEM((5, 2, 16, 256), F32), pltpu.VMEM((4, 5, 16, 128), F32),
            pltpu.VMEM(block, F32), pltpu.VMEM((TILES, 16, 256), F32),
            pltpu.VMEM((TILES, 16, 256), F32), pltpu.VMEM((16, 16, 128), F32),
            pltpu.VMEM((16, 128), F32), pltpu.VMEM((16, 128), F32),
            pltpu.VMEM(block, F32),
            dma((7,)), dma((17,)), dma((17,)),
        ],
        compiler_params=pltpu.CompilerParams(collective_id=0, has_side_effects=True),
    )(
        weights, perturb, coef_lon, coef_lat, obs_value, obs_weight,
        obs_segment.reshape(1, -1), obs_kind.reshape(1, -1), obs_target.reshape(1, -1),
        obs_count, operators,
    )
    return inc * scale, weights + (back * scale)[None]


def solution(mesh):
    placed = (
        P("mem", None, "tile", None),
        P("mem", None, "tile", None),
        P(None, "tile", None),
        P(None, "tile", None),
        P(("mem", "tile"), None),
        P(("mem", "tile"), None),
        P(("mem", "tile")),
        P(("mem", "tile")),
        P(("mem", "tile"), None),
        P(("mem", "tile")),
        P(),
    )
    return jax.shard_map(
        shards,
        mesh=mesh,
        in_specs=placed,
        out_specs=(P(None, "tile", None), P("mem", None, "tile", None)),
        check_vma=False,
    )
```

```python
import math

import jax
import jax.numpy as jnp
from jax import lax
from jax.experimental import pallas as pl
from jax.experimental.pallas import tpu as pltpu
from jax.sharding import PartitionSpec as P

SWEEPS = 16
AROUND = (5, 3, 7, 1, 4, 2, 6)
VMEM_LIMIT = 24 * 1024 * 1024
MEM = 32
TILES = 8
MESH = pl.DeviceIdType.MESH
HIGHEST = lax.Precision.HIGHEST
F32 = jnp.float32
BF16 = jnp.bfloat16


def eye_mask(n):
    return lax.broadcasted_iota(jnp.int32, (n, n), 0) == lax.broadcasted_iota(jnp.int32, (n, n), 1)


def column(row):
    return jnp.sum(jnp.where(eye_mask(row.shape[1]), row, 0.0), axis=1, keepdims=True)


def as_row(col):
    return jnp.sum(jnp.where(eye_mask(col.shape[0]), col, 0.0), axis=0, keepdims=True)


def split3(x):
    hi = x.astype(BF16)
    rest = x - hi.astype(F32)
    mid = rest.astype(BF16)
    low = (rest - mid.astype(F32)).astype(BF16)
    return jnp.concatenate([hi, mid, low], axis=1)


def select(onehot, parts):
    width = parts.shape[1] // 3
    got = jnp.dot(onehot.astype(BF16), parts, preferred_element_type=F32)
    return got[:, 0:width] + got[:, width:2 * width] + got[:, 2 * width:3 * width]


def aligned(index, size):
    return pl.ds(pl.multiple_of(index * size, size), size)


def kernel(
    cnt_ref, w_ref, p_ref, clon_ref, clat_ref, ov_hbm, ow_hbm, seg_hbm, kind_hbm, tgt_hbm, op_hbm,
    both_ref,
    wbuf, coef, pbuf, pf, pin, retain, ov_ref, ow_ref, op_ref, seg_ref, kind_ref, tgt_ref,
    pack, lists, ad, ybuf, s2, zbuf, prod, sibp, half, rs, inc_red, adj_red, fld,
    loc_sem, snd, rcv, list_rcv,
):
    inc_ref, back_ref = both_ref.at[0], both_ref.at[1]
    m = lax.axis_index("mem")
    t = lax.axis_index("tile")
    y = m // 8
    z = lax.rem(m // 2, 4)
    c = lax.rem(m, 2)
    sib = m + 1 - 2 * c
    place16 = m // 2
    scale = 1.0 / math.sqrt(MEM)
    lead = lax.rem(2 * y + z // 2 + t, TILES)
    cols = aligned(2 * c + lax.rem(z, 2), 128)

    def remote(src, dst, sem, member, tile):
        return pltpu.make_async_remote_copy(
            src_ref=src, dst_ref=dst, send_sem=snd.at[sem], recv_sem=rcv.at[sem],
            device_id=(member, tile), device_id_type=MESH,
        )

    def got(ref, sem):
        pltpu.make_async_copy(ref, ref, rcv.at[sem]).wait()

    def left(ref, sem):
        pltpu.make_async_copy(ref, ref, snd.at[sem]).wait()

    def greet(member, tile):
        pl.semaphore_signal(
            pltpu.get_barrier_semaphore(), inc=1, device_id=(member, tile), device_id_type=MESH
        )

    for d in range(1, TILES):
        greet(m, lax.rem(t + d, TILES))
    greet(sib, t)

    def greet_core(d, carry):
        greet(2 * lax.rem(place16 + d, 16) + c, t)
        return carry

    lax.fori_loop(1, 16, greet_core, 0)
    for source in range(4):
        tile = lax.rem(t + 2 * y + z // 2, TILES)

        @pl.when((tile != t) | (z != source))
        def _(source=source, tile=tile):
            greet(y * 8 + source * 2 + c, tile)

    piece = (aligned(c, 8), aligned(y, 128))
    loads = [
        pltpu.make_async_copy(seg_hbm, seg_ref, loc_sem.at[10]),
        pltpu.make_async_copy(kind_hbm, kind_ref, loc_sem.at[11]),
        pltpu.make_async_copy(tgt_hbm, tgt_ref, loc_sem.at[12]),
        pltpu.make_async_copy(op_hbm, op_ref, loc_sem.at[7]),
        pltpu.make_async_copy(ov_hbm, ov_ref, loc_sem.at[8]),
        pltpu.make_async_copy(ow_hbm, ow_ref, loc_sem.at[9]),
        pltpu.make_async_copy(p_ref.at[0], pin, loc_sem.at[0]),
    ]
    own = [
        pltpu.make_async_copy(clon_ref.at[(t,) + piece], coef.at[(0, t) + piece], loc_sem.at[2]),
        pltpu.make_async_copy(clat_ref.at[(t,) + piece], coef.at[(1, t) + piece], loc_sem.at[3]),
        pltpu.make_async_copy(w_ref.at[0, t], wbuf.at[t], loc_sem.at[1]),
    ]
    for copy in loads + own:
        copy.start()

    slots = ov_ref.shape[0]
    kinds = op_ref.shape[0]
    live = lax.broadcasted_iota(jnp.int32, (slots, 1), 0) < cnt_ref[0]
    lane = lax.broadcasted_iota(jnp.int32, (slots, 128), 1)
    for copy in loads[:3]:
        copy.wait()
    target = tgt_ref[...].astype(F32)
    seg_col = column(seg_ref[...].astype(F32))
    kind_col = column(kind_ref[...].astype(F32))
    named = (
        target == lax.broadcasted_iota(jnp.int32, (TILES, slots), 0).astype(F32)
    ).astype(F32)
    upper = (
        lax.broadcasted_iota(jnp.int32, (slots, slots), 0)
        < lax.broadcasted_iota(jnp.int32, (slots, slots), 1)
    ).astype(F32)
    earlier = jnp.dot(named, upper, preferred_element_type=F32)
    place = target * 16.0 + jnp.sum(earlier * named, axis=0, keepdims=True)
    route = (
        lax.broadcasted_iota(jnp.int32, (128, slots), 0).astype(F32) == place
    ).astype(F32)
    for copy in loads[3:]:
        copy.wait()
    flat = op_ref[...].reshape(kinds * 128, 128)
    precision = jnp.where(live, ow_ref[...], 0.0)
    weighted = precision * ov_ref[...]
    wide = jnp.concatenate(
        [jnp.where(kind_col == float(k), weighted, 0.0) for k in range(kinds)], axis=1
    )
    pulled = jnp.dot(wide, flat, precision=HIGHEST, preferred_element_type=F32)
    meta = jnp.where(lane == 0, seg_col, jnp.where(lane == 1, kind_col, 0.0))
    routed = select(route, split3(jnp.concatenate([pulled, precision, meta], axis=1)))
    pack[:, 0:16, :] = routed[:, 0:128].reshape(TILES, 16, 128)
    pack[:, 16:32, :] = routed[:, 128:256].reshape(TILES, 16, 128)
    routed_meta = routed[:, 256:384].reshape(TILES, 16, 128)
    pack[:, 32:40, :] = routed_meta[:, 0:8] + pltpu.roll(routed_meta[:, 8:16], 64, 2)
    pf[...] = pin[...].astype(F32)

    away = jnp.where((y == 0) & (z < 2), 3, 4)
    pl.semaphore_wait(pltpu.get_barrier_semaphore(), TILES - 1 + 1 + 15 + away)

    for d in AROUND:
        peer = lax.rem(t + d, TILES)
        remote(clon_ref.at[(peer,) + piece], coef.at[(0, t) + piece], 0, m, peer).start()
        remote(clat_ref.at[(peer,) + piece], coef.at[(1, t) + piece], 0, m, peer).start()
    for d in AROUND:
        peer = lax.rem(t + d, TILES)
        pltpu.make_async_remote_copy(
            src_ref=pack.at[peer], dst_ref=lists.at[c, t],
            send_sem=snd.at[1], recv_sem=list_rcv.at[d],
            device_id=(m, peer), device_id_type=MESH,
        ).start()
    own_o = pltpu.make_async_copy(pack.at[t], lists.at[c, t], loc_sem.at[5])
    own_o.start()
    for d in AROUND:
        peer = lax.rem(t + d, TILES)
        remote(w_ref.at[0, peer], wbuf.at[t], 2, m, peer).start()
    own[0].wait()
    own[1].wait()
    got(rs.at[pl.ds(0, 7)], 0)
    part = coef.at[(slice(None), slice(None)) + piece]
    for d in (2, 1, 3):
        remote(part, part, 4, lax.rem(y + d, 4) * 8 + z * 2 + c, t).start()

    own_o.wait()
    remote(lists.at[c, t], lists.at[c, t], 5, sib, t).start()
    for d in (4, 2, 6, 7, 1, 3, 5):
        source = lax.rem(t + TILES - d, TILES)
        block = lists.at[c, source]
        pltpu.make_async_copy(block, block, list_rcv.at[d]).wait()
        remote(block, block, 5, sib, t).start()

    for d in AROUND:
        peer = lax.rem(t + d, TILES)
        remote(pf.at[peer], pbuf.at[t], 3, m, peer).start()
    own_p = pltpu.make_async_copy(pf.at[t], pbuf.at[t], loc_sem.at[4])
    own_p.start()

    got(lists.at[0], 5)

    rows = lists[...].reshape(2 * TILES, 40, 128)
    pulled_parts = split3(rows[:, 0:16].reshape(256, 128))
    weight_parts = split3(rows[:, 16:32].reshape(256, 128))
    info = rows[:, 32:40]
    info = jnp.concatenate([info, pltpu.roll(info, 64, 2)], axis=1).reshape(256, 128)
    seg_row = as_row(info[:, 0:1])
    key_row = seg_row + 512.0 * as_row(info[:, 1:2])
    row = lax.broadcasted_iota(jnp.int32, (256, 256), 0)
    fixed = lax.rem(row, 16) * 4 + 2 * c + lax.rem(row // 32, 2)
    for d in (2, 1, 3, 0):
        there = lax.rem(y + d, 4)
        level = lax.rem(t - 2 * there - lax.rem(row // 16, 2) + TILES, TILES)
        cell = fixed + level * 64
        each = select(
            (key_row == (cell + (row // 64) * 512).astype(F32)).astype(F32), weight_parts
        ).reshape(kinds, 2, 2, 16, 128)
        every = select(
            (seg_row == cell[0:64].astype(F32)).astype(F32), pulled_parts
        ).reshape(2, 2, 16, 128)
        for b in range(2):
            span = pl.ds(b * 128, 128)
            for near in range(2):
                ad[d, near, 0:kinds, :, span] = each[:, b, near]
                ad[d, near, kinds, :, span] = every[b, near]
        if d:
            remote(ad.at[d, 0], ybuf.at[0, d - 1], 7, there * 8 + z * 2 + c, t).start()
    for d in (2, 1, 3):
        there = lax.rem(y + d, 4)
        remote(ad.at[d, 1], ybuf.at[1, d - 1], 17, there * 8 + z * 2 + c, t).start()

    got(wbuf.at[pl.ds(0, 6)], 4)
    rows8 = coef.at[:, :, piece[0], :]
    remote(rows8, rows8, 6, sib, t).start()

    got(rows8, 6)
    retain[...] = 1.0 - 2.0 * coef[0] - 2.0 * coef[1]

    own[2].wait()
    got(pf.at[pl.ds(0, 7)], 2)

    top = lax.broadcasted_iota(jnp.int32, (8, 512), 0) == 0
    bottom = lax.broadcasted_iota(jnp.int32, (8, 512), 0) == 7
    nothing = jnp.zeros((8, 512), F32)

    def block_of(i):
        return i // 2, pl.ds((i % 2) * 8, 8)

    def sweep(step, carry):
        here = wbuf[block_of(0)]
        down_before, up = nothing, pltpu.roll(here, 7, 0)
        for i in range(16):
            place = block_of(i)
            after = wbuf[block_of(i + 1)] if i < 15 else nothing
            down = pltpu.roll(here, 1, 0)
            up_after = pltpu.roll(after, 7, 0)
            across = jnp.where(top, down_before, down) + jnp.where(bottom, up_after, up)
            zonal = pltpu.roll(here, 1, 1) + pltpu.roll(here, 511, 1)
            wbuf[place] = (
                retain[place] * here + coef[(0,) + place] * zonal + coef[(1,) + place] * across
            )
            here, down_before, up = after, down, up_after
        return carry

    lax.fori_loop(0, SWEEPS, sweep, 0, unroll=4)
    def pass_on(near, sem):
        got(ybuf.at[near], sem)
        s2[near] = ad[0, near] + ybuf[near, 0] + ybuf[near, 1] + ybuf[near, 2]
        level_to = lax.rem(t - 2 * y - near + TILES, TILES)
        for b in range(2):
            tz = 2 * near + b
            block = s2.at[near, :, :, pl.ds(b * 128, 128)]
            self = (level_to == t) & (z == tz)

            @pl.when(self)
            def _(block=block):
                pltpu.make_async_copy(block, zbuf.at[z], rcv.at[10]).start()

            @pl.when(jnp.logical_not(self))
            def _(block=block, tz=tz):
                remote(block, zbuf.at[z], 10, y * 8 + tz * 2 + c, level_to).start()

    own_p.wait()
    got(pbuf.at[pl.ds(0, 7)], 3)
    prod[...] = wbuf[...] * pbuf[...]
    mine = aligned(c, 256)
    remote(prod.at[:, :, aligned(1 - c, 256)], sibp, 8, sib, t).start()

    pass_on(0, 7)
    got(sibp, 8)
    half[...] = prod[:, :, mine] + sibp[...]

    def scatter(d, carry):
        there = lax.rem(place16 + d, 16)
        ty = there // 4
        tz = lax.rem(there, 4)
        tlead = lax.rem(2 * ty + tz // 2 + t, TILES)
        remote(
            half.at[tlead, :, aligned(lax.rem(tz, 2), 128)], rs.at[d - 1], 9, 2 * there + c, t
        ).start()
        return carry

    lax.fori_loop(1, 16, scatter, 0)

    pass_on(1, 17)

    got(rs, 9)
    total = half[lead, :, aligned(lax.rem(z, 2), 128)] + jnp.sum(rs[...], axis=0)
    inc_red[...] = total

    got(zbuf, 10)
    normal = zbuf[0] + zbuf[1] + zbuf[2] + zbuf[3]
    images = lax.dot_general(
        total * scale, flat, (((1,), (1,)), ((), ())), precision=HIGHEST, preferred_element_type=F32
    )
    images = images * jnp.concatenate([normal[k] for k in range(kinds)], axis=1)
    adjoint = jnp.dot(images, flat, precision=HIGHEST, preferred_element_type=F32) - normal[kinds]
    adj_red[...] = adjoint


    def spread(d, carry):
        there = lax.rem(place16 + d, 16)
        remote(adj_red, fld.at[lead, :, cols], 11, 2 * there + c, t).start()
        return carry

    lax.fori_loop(1, 16, spread, 0)
    fld[lead, :, cols] = adjoint
    got(rs, 11)
    side = fld.at[:, :, mine]
    remote(side, side, 12, sib, t).start()

    def tell(d, carry):
        there = lax.rem(place16 + d, 16)
        remote(inc_red, inc_ref.at[t, :, cols], 13, 2 * there + c, lead).start()
        return carry

    lax.fori_loop(1, 16, tell, 0)
    far = remote(inc_red, inc_ref.at[t, :, cols], 14, m, lead)

    @pl.when(lead == t)
    def _():
        pltpu.make_async_copy(inc_red, inc_ref.at[t, :, cols], rcv.at[14]).start()

    @pl.when(lead != t)
    def _():
        far.start()

    got(side, 12)

    left(sibp, 8)
    prod[...] = fld[...] * pbuf[...]

    def sweep_back(step, carry):
        here = prod[block_of(0)]
        flux = coef[(1,) + block_of(0)] * here
        down_before, up = nothing, pltpu.roll(flux, 7, 0)
        for i in range(16):
            place = block_of(i)
            if i < 15:
                after = prod[block_of(i + 1)]
                flux_after = coef[(1,) + block_of(i + 1)] * after
            else:
                after = flux_after = nothing
            down = pltpu.roll(flux, 1, 0)
            up_after = pltpu.roll(flux_after, 7, 0)
            across = jnp.where(top, down_before, down) + jnp.where(bottom, up_after, up)
            flux_lon = coef[(0,) + place] * here
            prod[place] = (
                retain[place] * here
                + (pltpu.roll(flux_lon, 1, 1) + pltpu.roll(flux_lon, 511, 1))
                + across
            )
            here, flux, down_before, up = after, flux_after, down, up_after
        return carry

    lax.fori_loop(0, SWEEPS, sweep_back, 0, unroll=4)
    for d in AROUND:
        peer = lax.rem(t + d, TILES)
        remote(prod.at[peer], back_ref.at[t], 15, m, peer).start()
    own_b = pltpu.make_async_copy(prod.at[t], back_ref.at[t], loc_sem.at[6])
    own_b.start()

    got(rs, 13)
    got(inc_red, 14)
    side_inc = inc_ref.at[:, :, mine]
    remote(side_inc, side_inc, 16, sib, t).start()

    own_b.wait()
    got(prod.at[pl.ds(0, 7)], 15)
    got(side_inc, 16)
    left(rs.at[pl.ds(0, 7)], 0)
    left(pack.at[pl.ds(0, 7)], 1)
    left(wbuf.at[pl.ds(0, 7)], 2)
    left(pf.at[pl.ds(0, 7)], 3)
    left(wbuf.at[pl.ds(0, 6)], 4)
    left(lists.at[0], 5)
    left(rows8, 6)
    left(ybuf.at[0], 7)
    left(ybuf.at[1], 17)
    left(rs, 9)

    @pl.when((y == 0) & (z < 2))
    def _():
        left(zbuf.at[pl.ds(0, 3)], 10)

    @pl.when((y > 0) | (z >= 2))
    def _():
        left(zbuf, 10)

    left(rs, 11)
    left(side, 12)
    left(rs, 13)

    @pl.when(lead != t)
    def _():
        far.wait_send()

    left(prod.at[pl.ds(0, 7)], 15)
    left(side_inc, 16)


def shards(
    weights, perturb, coef_lon, coef_lat, obs_value, obs_weight,
    obs_segment, obs_kind, obs_target, obs_count, operators,
):
    scale = 1.0 / math.sqrt(MEM)
    hbm = pl.BlockSpec(memory_space=pl.ANY)
    smem = pl.BlockSpec(memory_space=pltpu.SMEM)
    block = (TILES, 16, 512)
    dma = pltpu.SemaphoreType.DMA
    far = pl.BlockSpec(memory_space=pltpu.HBM)
    given = [
        pltpu.with_memory_space_constraint(a, pltpu.HBM)
        for a in (
            weights, perturb, coef_lon, coef_lat, obs_value, obs_weight,
            obs_segment.reshape(1, -1), obs_kind.reshape(1, -1), obs_target.reshape(1, -1), operators,
        )
    ]
    both = pl.pallas_call(
        kernel,
        out_shape=jax.ShapeDtypeStruct((2,) + block, F32),
        in_specs=[smem] + [far] * len(given),
        out_specs=hbm,
        scratch_shapes=[
            pltpu.VMEM(block, F32), pltpu.VMEM((2,) + block, F32),
            pltpu.VMEM(block, F32), pltpu.VMEM(block, F32), pltpu.VMEM(block, BF16),
            pltpu.VMEM(block, F32), pltpu.VMEM(obs_value.shape, F32),
            pltpu.VMEM(obs_weight.shape, F32), pltpu.VMEM(operators.shape, F32),
            pltpu.VMEM((1, obs_segment.shape[0]), jnp.int32),
            pltpu.VMEM((1, obs_kind.shape[0]), jnp.int32),
            pltpu.VMEM((1, obs_target.shape[0]), jnp.int32),
            pltpu.VMEM((TILES, 40, 128), F32), pltpu.VMEM((2, TILES, 40, 128), F32),
            pltpu.VMEM((4, 2, 5, 16, 256), F32), pltpu.VMEM((2, 3, 5, 16, 256), F32),
            pltpu.VMEM((2, 5, 16, 256), F32), pltpu.VMEM((4, 5, 16, 128), F32),
            pltpu.VMEM(block, F32), pltpu.VMEM((TILES, 16, 256), F32),
            pltpu.VMEM((TILES, 16, 256), F32), pltpu.VMEM((15, 16, 128), F32),
            pltpu.VMEM((16, 128), F32), pltpu.VMEM((16, 128), F32),
            pltpu.VMEM(block, F32),
            dma((13,)), dma((18,)), dma((18,)), dma((TILES,)),
        ],
        compiler_params=pltpu.CompilerParams(
            collective_id=0, has_side_effects=True, vmem_limit_bytes=VMEM_LIMIT
        ),
    )(obs_count, *given)
    return both[0] * scale, weights + (both[1] * scale)[None]


def solution(mesh):
    placed = (
        P("mem", None, "tile", None),
        P("mem", None, "tile", None),
        P(None, "tile", None),
        P(None, "tile", None),
        P(("mem", "tile"), None),
        P(("mem", "tile"), None),
        P(("mem", "tile")),
        P(("mem", "tile")),
        P(("mem", "tile"), None),
        P(("mem", "tile")),
        P(),
    )
    return jax.shard_map(
        shards,
        mesh=mesh,
        in_specs=placed,
        out_specs=(P(None, "tile", None), P("mem", None, "tile", None)),
        check_vma=False,
    )
```

```python
import math

import jax
import jax.numpy as jnp
from jax import lax
from jax.experimental import pallas as pl
from jax.experimental.pallas import tpu as pltpu
from jax.sharding import PartitionSpec as P

SWEEPS = 16
AROUND = (5, 3, 7, 1, 4, 2, 6)
VMEM_LIMIT = 24 * 1024 * 1024
MEM = 32
TILES = 8
MESH = pl.DeviceIdType.MESH
HIGHEST = lax.Precision.HIGHEST
F32 = jnp.float32
BF16 = jnp.bfloat16


def eye_mask(n):
    return lax.broadcasted_iota(jnp.int32, (n, n), 0) == lax.broadcasted_iota(jnp.int32, (n, n), 1)


def column(row):
    return jnp.sum(jnp.where(eye_mask(row.shape[1]), row, 0.0), axis=1, keepdims=True)


def as_row(col):
    return jnp.sum(jnp.where(eye_mask(col.shape[0]), col, 0.0), axis=0, keepdims=True)


def split3(x):
    hi = x.astype(BF16)
    rest = x - hi.astype(F32)
    mid = rest.astype(BF16)
    low = (rest - mid.astype(F32)).astype(BF16)
    return jnp.concatenate([hi, mid, low], axis=1)


def select(onehot, parts):
    width = parts.shape[1] // 3
    got = jnp.dot(onehot.astype(BF16), parts, preferred_element_type=F32)
    return got[:, 0:width] + got[:, width:2 * width] + got[:, 2 * width:3 * width]


def aligned(index, size):
    return pl.ds(pl.multiple_of(index * size, size), size)


def kernel(
    cnt_ref, w_ref, p_ref, clon_ref, clat_ref, ov_hbm, ow_hbm, seg_hbm, kind_hbm, tgt_hbm, op_hbm,
    both_ref,
    wbuf, coef, pbuf, pf, pin, retain, ov_ref, ow_ref, op_ref, seg_ref, kind_ref, tgt_ref,
    pack, lists, ad, ybuf, s2, zbuf, prod, sibp, half, rsy, sumy, rsz, rs, inc_red, adj_red, fld,
    loc_sem, snd, rcv, list_rcv,
):
    inc_ref, back_ref = both_ref.at[0], both_ref.at[1]
    m = lax.axis_index("mem")
    t = lax.axis_index("tile")
    y = m // 8
    z = lax.rem(m // 2, 4)
    c = lax.rem(m, 2)
    sib = m + 1 - 2 * c
    place16 = m // 2
    scale = 1.0 / math.sqrt(MEM)
    lead = lax.rem(2 * y + z // 2 + t, TILES)
    cols = aligned(2 * c + lax.rem(z, 2), 128)

    def remote(src, dst, sem, member, tile):
        return pltpu.make_async_remote_copy(
            src_ref=src, dst_ref=dst, send_sem=snd.at[sem], recv_sem=rcv.at[sem],
            device_id=(member, tile), device_id_type=MESH,
        )

    def got(ref, sem):
        pltpu.make_async_copy(ref, ref, rcv.at[sem]).wait()

    def left(ref, sem):
        pltpu.make_async_copy(ref, ref, snd.at[sem]).wait()

    def greet(member, tile):
        pl.semaphore_signal(
            pltpu.get_barrier_semaphore(), inc=1, device_id=(member, tile), device_id_type=MESH
        )

    for d in range(1, TILES):
        greet(m, lax.rem(t + d, TILES))
    greet(sib, t)

    def greet_core(d, carry):
        greet(2 * lax.rem(place16 + d, 16) + c, t)
        return carry

    lax.fori_loop(1, 16, greet_core, 0)
    for source in range(4):
        tile = lax.rem(t + 2 * y + z // 2, TILES)

        @pl.when((tile != t) | (z != source))
        def _(source=source, tile=tile):
            greet(y * 8 + source * 2 + c, tile)

    piece = (aligned(c, 8), aligned(y, 128))
    loads = [
        pltpu.make_async_copy(seg_hbm, seg_ref, loc_sem.at[10]),
        pltpu.make_async_copy(kind_hbm, kind_ref, loc_sem.at[11]),
        pltpu.make_async_copy(tgt_hbm, tgt_ref, loc_sem.at[12]),
        pltpu.make_async_copy(op_hbm, op_ref, loc_sem.at[7]),
        pltpu.make_async_copy(ov_hbm, ov_ref, loc_sem.at[8]),
        pltpu.make_async_copy(ow_hbm, ow_ref, loc_sem.at[9]),
        pltpu.make_async_copy(p_ref.at[0], pin, loc_sem.at[0]),
    ]
    own = [
        pltpu.make_async_copy(clon_ref.at[(t,) + piece], coef.at[(0, t) + piece], loc_sem.at[2]),
        pltpu.make_async_copy(clat_ref.at[(t,) + piece], coef.at[(1, t) + piece], loc_sem.at[3]),
        pltpu.make_async_copy(w_ref.at[0, t], wbuf.at[t], loc_sem.at[1]),
    ]
    for copy in loads + own:
        copy.start()

    slots = ov_ref.shape[0]
    kinds = op_ref.shape[0]
    live = lax.broadcasted_iota(jnp.int32, (slots, 1), 0) < cnt_ref[0]
    lane = lax.broadcasted_iota(jnp.int32, (slots, 128), 1)
    for copy in loads[:3]:
        copy.wait()
    target = tgt_ref[...].astype(F32)
    seg_col = column(seg_ref[...].astype(F32))
    kind_col = column(kind_ref[...].astype(F32))
    named = (
        target == lax.broadcasted_iota(jnp.int32, (TILES, slots), 0).astype(F32)
    ).astype(F32)
    upper = (
        lax.broadcasted_iota(jnp.int32, (slots, slots), 0)
        < lax.broadcasted_iota(jnp.int32, (slots, slots), 1)
    ).astype(F32)
    earlier = jnp.dot(named, upper, preferred_element_type=F32)
    place = target * 16.0 + jnp.sum(earlier * named, axis=0, keepdims=True)
    route = (
        lax.broadcasted_iota(jnp.int32, (128, slots), 0).astype(F32) == place
    ).astype(F32)
    for copy in loads[3:]:
        copy.wait()
    flat = op_ref[...].reshape(kinds * 128, 128)
    precision = jnp.where(live, ow_ref[...], 0.0)
    weighted = precision * ov_ref[...]
    wide = jnp.concatenate(
        [jnp.where(kind_col == float(k), weighted, 0.0) for k in range(kinds)], axis=1
    )
    pulled = jnp.dot(wide, flat, precision=HIGHEST, preferred_element_type=F32)
    meta = jnp.where(lane == 0, seg_col, jnp.where(lane == 1, kind_col, 0.0))
    routed = select(route, split3(jnp.concatenate([pulled, precision, meta], axis=1)))
    pack[:, 0:16, :] = routed[:, 0:128].reshape(TILES, 16, 128)
    pack[:, 16:32, :] = routed[:, 128:256].reshape(TILES, 16, 128)
    routed_meta = routed[:, 256:384].reshape(TILES, 16, 128)
    pack[:, 32:40, :] = routed_meta[:, 0:8] + pltpu.roll(routed_meta[:, 8:16], 64, 2)
    pf[...] = pin[...].astype(F32)

    away = jnp.where((y == 0) & (z < 2), 3, 4)
    pl.semaphore_wait(pltpu.get_barrier_semaphore(), TILES - 1 + 1 + 15 + away)

    for d in AROUND:
        peer = lax.rem(t + d, TILES)
        remote(clon_ref.at[(peer,) + piece], coef.at[(0, t) + piece], 0, m, peer).start()
        remote(clat_ref.at[(peer,) + piece], coef.at[(1, t) + piece], 0, m, peer).start()
    for d in AROUND:
        peer = lax.rem(t + d, TILES)
        pltpu.make_async_remote_copy(
            src_ref=pack.at[peer], dst_ref=lists.at[c, t],
            send_sem=snd.at[1], recv_sem=list_rcv.at[d],
            device_id=(m, peer), device_id_type=MESH,
        ).start()
    own_o = pltpu.make_async_copy(pack.at[t], lists.at[c, t], loc_sem.at[5])
    own_o.start()
    for d in AROUND:
        peer = lax.rem(t + d, TILES)
        remote(w_ref.at[0, peer], wbuf.at[t], 2, m, peer).start()
    own[0].wait()
    own[1].wait()
    got(rs.at[pl.ds(0, 7)], 0)
    part = coef.at[(slice(None), slice(None)) + piece]
    for d in (2, 1, 3):
        remote(part, part, 4, lax.rem(y + d, 4) * 8 + z * 2 + c, t).start()

    own_o.wait()
    remote(lists.at[c, t], lists.at[c, t], 5, sib, t).start()
    for d in (4, 2, 6, 7, 1, 3, 5):
        source = lax.rem(t + TILES - d, TILES)
        block = lists.at[c, source]
        pltpu.make_async_copy(block, block, list_rcv.at[d]).wait()
        remote(block, block, 5, sib, t).start()

    for d in AROUND:
        peer = lax.rem(t + d, TILES)
        remote(pf.at[peer], pbuf.at[t], 3, m, peer).start()
    own_p = pltpu.make_async_copy(pf.at[t], pbuf.at[t], loc_sem.at[4])
    own_p.start()

    got(lists.at[0], 5)

    rows = lists[...].reshape(2 * TILES, 40, 128)
    pulled_parts = split3(rows[:, 0:16].reshape(256, 128))
    weight_parts = split3(rows[:, 16:32].reshape(256, 128))
    info = rows[:, 32:40]
    info = jnp.concatenate([info, pltpu.roll(info, 64, 2)], axis=1).reshape(256, 128)
    seg_row = as_row(info[:, 0:1])
    key_row = seg_row + 512.0 * as_row(info[:, 1:2])
    row = lax.broadcasted_iota(jnp.int32, (256, 256), 0)
    fixed = lax.rem(row, 16) * 4 + 2 * c + lax.rem(row // 32, 2)
    for d in (2, 1, 3, 0):
        there = lax.rem(y + d, 4)
        level = lax.rem(t - 2 * there - lax.rem(row // 16, 2) + TILES, TILES)
        cell = fixed + level * 64
        each = select(
            (key_row == (cell + (row // 64) * 512).astype(F32)).astype(F32), weight_parts
        ).reshape(kinds, 2, 2, 16, 128)
        every = select(
            (seg_row == cell[0:64].astype(F32)).astype(F32), pulled_parts
        ).reshape(2, 2, 16, 128)
        for b in range(2):
            span = pl.ds(b * 128, 128)
            for near in range(2):
                ad[d, near, 0:kinds, :, span] = each[:, b, near]
                ad[d, near, kinds, :, span] = every[b, near]
        if d:
            remote(ad.at[d, 0], ybuf.at[0, d - 1], 7, there * 8 + z * 2 + c, t).start()
    for d in (2, 1, 3):
        there = lax.rem(y + d, 4)
        remote(ad.at[d, 1], ybuf.at[1, d - 1], 17, there * 8 + z * 2 + c, t).start()

    got(wbuf.at[pl.ds(0, 6)], 4)
    rows8 = coef.at[:, :, piece[0], :]
    remote(rows8, rows8, 6, sib, t).start()

    got(rows8, 6)
    retain[...] = 1.0 - 2.0 * coef[0] - 2.0 * coef[1]

    own[2].wait()
    got(pf.at[pl.ds(0, 7)], 2)

    top = lax.broadcasted_iota(jnp.int32, (8, 512), 0) == 0
    bottom = lax.broadcasted_iota(jnp.int32, (8, 512), 0) == 7
    nothing = jnp.zeros((8, 512), F32)

    def block_of(i):
        return i // 2, pl.ds((i % 2) * 8, 8)

    def sweep(step, carry):
        here = wbuf[block_of(0)]
        down_before, up = nothing, pltpu.roll(here, 7, 0)
        for i in range(16):
            place = block_of(i)
            after = wbuf[block_of(i + 1)] if i < 15 else nothing
            down = pltpu.roll(here, 1, 0)
            up_after = pltpu.roll(after, 7, 0)
            across = jnp.where(top, down_before, down) + jnp.where(bottom, up_after, up)
            zonal = pltpu.roll(here, 1, 1) + pltpu.roll(here, 511, 1)
            wbuf[place] = (
                retain[place] * here + coef[(0,) + place] * zonal + coef[(1,) + place] * across
            )
            here, down_before, up = after, down, up_after
        return carry

    lax.fori_loop(0, SWEEPS, sweep, 0, unroll=4)
    def pass_on(near, sem):
        got(ybuf.at[near], sem)
        s2[near] = ad[0, near] + ybuf[near, 0] + ybuf[near, 1] + ybuf[near, 2]
        level_to = lax.rem(t - 2 * y - near + TILES, TILES)
        for b in range(2):
            tz = 2 * near + b
            block = s2.at[near, :, :, pl.ds(b * 128, 128)]
            self = (level_to == t) & (z == tz)

            @pl.when(self)
            def _(block=block):
                pltpu.make_async_copy(block, zbuf.at[z], rcv.at[10]).start()

            @pl.when(jnp.logical_not(self))
            def _(block=block, tz=tz):
                remote(block, zbuf.at[z], 10, y * 8 + tz * 2 + c, level_to).start()

    own_p.wait()
    got(pbuf.at[pl.ds(0, 7)], 3)
    prod[...] = wbuf[...] * pbuf[...]
    mine = aligned(c, 256)
    remote(prod.at[:, :, aligned(1 - c, 256)], sibp, 8, sib, t).start()

    pass_on(0, 7)
    got(sibp, 8)
    for near in range(8):
        tile_to = lax.rem(near + t, TILES)
        half[near] = prod[tile_to, :, mine] + sibp[tile_to]
    for d in (2, 1, 3):
        there = lax.rem(y + d, 4)
        remote(half.at[pl.ds(2 * there, 2)], rsy.at[d - 1], 9, there * 8 + z * 2 + c, t).start()

    pass_on(1, 17)

    got(rsy, 9)
    sumy[...] = half[pl.ds(2 * y, 2)] + rsy[0] + rsy[1] + rsy[2]
    for d in (2, 1, 3):
        tz = lax.rem(z + d, 4)
        remote(
            sumy.at[tz // 2, :, aligned(lax.rem(tz, 2), 128)], rsz.at[d - 1], 18,
            y * 8 + tz * 2 + c, t,
        ).start()
    got(rsz, 18)
    total = sumy[z // 2, :, aligned(lax.rem(z, 2), 128)] + rsz[0] + rsz[1] + rsz[2]
    inc_red[...] = total

    got(zbuf, 10)
    normal = zbuf[0] + zbuf[1] + zbuf[2] + zbuf[3]
    images = lax.dot_general(
        total * scale, flat, (((1,), (1,)), ((), ())), precision=HIGHEST, preferred_element_type=F32
    )
    images = images * jnp.concatenate([normal[k] for k in range(kinds)], axis=1)
    adjoint = jnp.dot(images, flat, precision=HIGHEST, preferred_element_type=F32) - normal[kinds]
    adj_red[...] = adjoint


    def spread(d, carry):
        there = lax.rem(place16 + d, 16)
        remote(adj_red, fld.at[lead, :, cols], 11, 2 * there + c, t).start()
        return carry

    lax.fori_loop(1, 16, spread, 0)
    fld[lead, :, cols] = adjoint
    for d in (2, 1, 3):
        tz = lax.rem(z + d, 4)
        remote(inc_red, inc_ref.at[t, :, cols], 13, y * 8 + tz * 2 + c, lead).start()
    far = remote(inc_red, inc_ref.at[t, :, cols], 14, m, lead)

    @pl.when(lead == t)
    def _():
        pltpu.make_async_copy(inc_red, inc_ref.at[t, :, cols], rcv.at[14]).start()

    @pl.when(lead != t)
    def _():
        far.start()

    got(rs, 11)
    side = fld.at[:, :, mine]
    remote(side, side, 12, sib, t).start()

    got(side, 12)

    left(sibp, 8)
    prod[...] = fld[...] * pbuf[...]

    def sweep_back(step, carry):
        here = prod[block_of(0)]
        flux = coef[(1,) + block_of(0)] * here
        down_before, up = nothing, pltpu.roll(flux, 7, 0)
        for i in range(16):
            place = block_of(i)
            if i < 15:
                after = prod[block_of(i + 1)]
                flux_after = coef[(1,) + block_of(i + 1)] * after
            else:
                after = flux_after = nothing
            down = pltpu.roll(flux, 1, 0)
            up_after = pltpu.roll(flux_after, 7, 0)
            across = jnp.where(top, down_before, down) + jnp.where(bottom, up_after, up)
            flux_lon = coef[(0,) + place] * here
            prod[place] = (
                retain[place] * here
                + (pltpu.roll(flux_lon, 1, 1) + pltpu.roll(flux_lon, 511, 1))
                + across
            )
            here, flux, down_before, up = after, flux_after, down, up_after
        return carry

    lax.fori_loop(0, SWEEPS, sweep_back, 0, unroll=4)
    for d in AROUND:
        peer = lax.rem(t + d, TILES)
        remote(prod.at[peer], back_ref.at[t], 15, m, peer).start()
    own_b = pltpu.make_async_copy(prod.at[t], back_ref.at[t], loc_sem.at[6])
    own_b.start()

    got(rsz, 13)
    got(inc_red, 14)
    for near in range(2):
        block = inc_ref.at[lax.rem(t - 2 * y - near + TILES, TILES), :, mine]
        for d in (2, 1, 3):
            remote(block, block, 19, lax.rem(y + d, 4) * 8 + z * 2 + c, t).start()
    got(half.at[pl.ds(0, 6)], 19)
    side_inc = inc_ref.at[:, :, mine]
    remote(side_inc, side_inc, 16, sib, t).start()

    own_b.wait()
    got(prod.at[pl.ds(0, 7)], 15)
    got(side_inc, 16)
    left(rs.at[pl.ds(0, 7)], 0)
    left(pack.at[pl.ds(0, 7)], 1)
    left(wbuf.at[pl.ds(0, 7)], 2)
    left(pf.at[pl.ds(0, 7)], 3)
    left(wbuf.at[pl.ds(0, 6)], 4)
    left(lists.at[0], 5)
    left(rows8, 6)
    left(ybuf.at[0], 7)
    left(ybuf.at[1], 17)
    left(rsy, 9)
    left(rsz, 18)

    @pl.when((y == 0) & (z < 2))
    def _():
        left(zbuf.at[pl.ds(0, 3)], 10)

    @pl.when((y > 0) | (z >= 2))
    def _():
        left(zbuf, 10)

    left(rs, 11)
    left(side, 12)
    left(rsz, 13)
    left(half.at[pl.ds(0, 6)], 19)

    @pl.when(lead != t)
    def _():
        far.wait_send()

    left(prod.at[pl.ds(0, 7)], 15)
    left(side_inc, 16)


def shards(
    weights, perturb, coef_lon, coef_lat, obs_value, obs_weight,
    obs_segment, obs_kind, obs_target, obs_count, operators,
):
    scale = 1.0 / math.sqrt(MEM)
    hbm = pl.BlockSpec(memory_space=pl.ANY)
    smem = pl.BlockSpec(memory_space=pltpu.SMEM)
    block = (TILES, 16, 512)
    dma = pltpu.SemaphoreType.DMA
    far = pl.BlockSpec(memory_space=pltpu.HBM)
    given = [
        pltpu.with_memory_space_constraint(a, pltpu.HBM)
        for a in (
            weights, perturb, coef_lon, coef_lat, obs_value, obs_weight,
            obs_segment.reshape(1, -1), obs_kind.reshape(1, -1), obs_target.reshape(1, -1), operators,
        )
    ]
    both = pl.pallas_call(
        kernel,
        out_shape=jax.ShapeDtypeStruct((2,) + block, F32),
        in_specs=[smem] + [far] * len(given),
        out_specs=hbm,
        scratch_shapes=[
            pltpu.VMEM(block, F32), pltpu.VMEM((2,) + block, F32),
            pltpu.VMEM(block, F32), pltpu.VMEM(block, F32), pltpu.VMEM(block, BF16),
            pltpu.VMEM(block, F32), pltpu.VMEM(obs_value.shape, F32),
            pltpu.VMEM(obs_weight.shape, F32), pltpu.VMEM(operators.shape, F32),
            pltpu.VMEM((1, obs_segment.shape[0]), jnp.int32),
            pltpu.VMEM((1, obs_kind.shape[0]), jnp.int32),
            pltpu.VMEM((1, obs_target.shape[0]), jnp.int32),
            pltpu.VMEM((TILES, 40, 128), F32), pltpu.VMEM((2, TILES, 40, 128), F32),
            pltpu.VMEM((4, 2, 5, 16, 256), F32), pltpu.VMEM((2, 3, 5, 16, 256), F32),
            pltpu.VMEM((2, 5, 16, 256), F32), pltpu.VMEM((4, 5, 16, 128), F32),
            pltpu.VMEM(block, F32), pltpu.VMEM((TILES, 16, 256), F32),
            pltpu.VMEM((TILES, 16, 256), F32), pltpu.VMEM((3, 2, 16, 256), F32),
            pltpu.VMEM((2, 16, 256), F32), pltpu.VMEM((3, 16, 128), F32),
            pltpu.VMEM((15, 16, 128), F32),
            pltpu.VMEM((16, 128), F32), pltpu.VMEM((16, 128), F32),
            pltpu.VMEM(block, F32),
            dma((13,)), dma((20,)), dma((20,)), dma((TILES,)),
        ],
        compiler_params=pltpu.CompilerParams(
            collective_id=0, has_side_effects=True, vmem_limit_bytes=VMEM_LIMIT
        ),
    )(obs_count, *given)
    return both[0] * scale, weights + (both[1] * scale)[None]


def solution(mesh):
    placed = (
        P("mem", None, "tile", None),
        P("mem", None, "tile", None),
        P(None, "tile", None),
        P(None, "tile", None),
        P(("mem", "tile"), None),
        P(("mem", "tile"), None),
        P(("mem", "tile")),
        P(("mem", "tile")),
        P(("mem", "tile"), None),
        P(("mem", "tile")),
        P(),
    )
    return jax.shard_map(
        shards,
        mesh=mesh,
        in_specs=placed,
        out_specs=(P(None, "tile", None), P("mem", None, "tile", None)),
        check_vma=False,
    )
```

```python
import math

import jax
import jax.numpy as jnp
from jax import lax
from jax.experimental import pallas as pl
from jax.experimental.pallas import tpu as pltpu
from jax.sharding import PartitionSpec as P

SWEEPS = 16
NAMES = 20
AROUND = (5, 3, 7, 1, 4, 2, 6)
VMEM_LIMIT = 24 * 1024 * 1024
MEM = 32
TILES = 8
MESH = pl.DeviceIdType.MESH
HIGHEST = lax.Precision.HIGHEST
F32 = jnp.float32
BF16 = jnp.bfloat16


def eye_mask(n):
    return lax.broadcasted_iota(jnp.int32, (n, n), 0) == lax.broadcasted_iota(jnp.int32, (n, n), 1)


def column(row):
    return jnp.sum(jnp.where(eye_mask(row.shape[1]), row, 0.0), axis=1, keepdims=True)


def as_row(col):
    return jnp.sum(jnp.where(eye_mask(col.shape[0]), col, 0.0), axis=0, keepdims=True)


def split3(x):
    hi = x.astype(BF16)
    rest = x - hi.astype(F32)
    mid = rest.astype(BF16)
    low = (rest - mid.astype(F32)).astype(BF16)
    return jnp.concatenate([hi, mid, low], axis=1)


def select(onehot, parts):
    width = parts.shape[1] // 3
    got = jnp.dot(onehot.astype(BF16), parts, preferred_element_type=F32)
    return got[:, 0:width] + got[:, width:2 * width] + got[:, 2 * width:3 * width]


def aligned(index, size):
    return pl.ds(pl.multiple_of(index * size, size), size)


def kernel(
    cnt_ref, w_ref, p_ref, clon_ref, clat_ref, ov_hbm, ow_hbm, seg_hbm, kind_hbm, tgt_hbm, op_hbm,
    both_ref,
    wbuf, coef, pbuf, pf, pin, retain, ov_ref, ow_ref, op_ref, seg_ref, kind_ref, tgt_ref,
    pack, lists, names, named_in, ad, ybuf, s2, zbuf, prod, sibp, half, rsy, sumy, rsz, rs, inc_red, adj_red, fld,
    loc_sem, snd, rcv, list_rcv,
):
    inc_ref, back_ref = both_ref.at[0], both_ref.at[1]
    m = lax.axis_index("mem")
    t = lax.axis_index("tile")
    y = m // 8
    z = lax.rem(m // 2, 4)
    c = lax.rem(m, 2)
    sib = m + 1 - 2 * c
    place16 = m // 2
    scale = 1.0 / math.sqrt(MEM)
    lead = lax.rem(2 * y + z // 2 + t, TILES)
    cols = aligned(2 * c + lax.rem(z, 2), 128)

    def remote(src, dst, sem, member, tile):
        return pltpu.make_async_remote_copy(
            src_ref=src, dst_ref=dst, send_sem=snd.at[sem], recv_sem=rcv.at[sem],
            device_id=(member, tile), device_id_type=MESH,
        )

    def got(ref, sem):
        pltpu.make_async_copy(ref, ref, rcv.at[sem]).wait()

    def left(ref, sem):
        pltpu.make_async_copy(ref, ref, snd.at[sem]).wait()

    def greet(member, tile):
        pl.semaphore_signal(
            pltpu.get_barrier_semaphore(), inc=1, device_id=(member, tile), device_id_type=MESH
        )

    for d in range(1, TILES):
        greet(m, lax.rem(t + d, TILES))
    greet(sib, t)

    def greet_core(d, carry):
        greet(2 * lax.rem(place16 + d, 16) + c, t)
        return carry

    lax.fori_loop(1, 16, greet_core, 0)
    for source in range(4):
        tile = lax.rem(t + 2 * y + z // 2, TILES)

        @pl.when((tile != t) | (z != source))
        def _(source=source, tile=tile):
            greet(y * 8 + source * 2 + c, tile)

    piece = (aligned(c, 8), aligned(y, 128))
    loads = [
        pltpu.make_async_copy(seg_hbm, seg_ref, loc_sem.at[10]),
        pltpu.make_async_copy(kind_hbm, kind_ref, loc_sem.at[11]),
        pltpu.make_async_copy(tgt_hbm, tgt_ref, loc_sem.at[12]),
        pltpu.make_async_copy(op_hbm, op_ref, loc_sem.at[7]),
        pltpu.make_async_copy(ov_hbm, ov_ref, loc_sem.at[8]),
        pltpu.make_async_copy(ow_hbm, ow_ref, loc_sem.at[9]),
        pltpu.make_async_copy(p_ref.at[0], pin, loc_sem.at[0]),
    ]
    own = [
        pltpu.make_async_copy(clon_ref.at[(t,) + piece], coef.at[(0, t) + piece], loc_sem.at[2]),
        pltpu.make_async_copy(clat_ref.at[(t,) + piece], coef.at[(1, t) + piece], loc_sem.at[3]),
        pltpu.make_async_copy(w_ref.at[0, t], wbuf.at[t], loc_sem.at[1]),
    ]
    for copy in loads + own:
        copy.start()

    slots = ov_ref.shape[0]
    kinds = op_ref.shape[0]
    live = lax.broadcasted_iota(jnp.int32, (slots, 1), 0) < cnt_ref[0]
    for copy in loads[:3]:
        copy.wait()
    target = tgt_ref[...].astype(F32)
    seg_row = seg_ref[...].astype(F32)
    kind_row = kind_ref[...].astype(F32)
    kind_col = column(kind_row)
    named = (
        target == lax.broadcasted_iota(jnp.int32, (TILES, slots), 0).astype(F32)
    ).astype(F32)
    upper = (
        lax.broadcasted_iota(jnp.int32, (slots, slots), 0)
        < lax.broadcasted_iota(jnp.int32, (slots, slots), 1)
    ).astype(F32)
    earlier = jnp.dot(named, upper, preferred_element_type=F32)
    rank = jnp.sum(earlier * named, axis=0, keepdims=True)
    place = target * 16.0 + rank
    at_lane = (
        column(rank) == lax.rem(lax.broadcasted_iota(jnp.int32, (slots, 128), 1), 16).astype(F32)
    ).astype(F32)
    told = jnp.dot(
        jnp.concatenate([named * seg_row, named * kind_row], axis=0), at_lane,
        precision=HIGHEST, preferred_element_type=F32,
    )
    for k in range(TILES):
        names[k, 0:1] = told[k:k + 1]
        names[k, 1:2] = told[TILES + k:TILES + k + 1]
    route = (
        lax.broadcasted_iota(jnp.int32, (128, slots), 0).astype(F32) == place
    ).astype(F32)
    for copy in loads[3:]:
        copy.wait()
    flat = op_ref[...].reshape(kinds * 128, 128)
    precision = jnp.where(live, ow_ref[...], 0.0)
    weighted = precision * ov_ref[...]
    wide = jnp.concatenate(
        [jnp.where(kind_col == float(k), weighted, 0.0) for k in range(kinds)], axis=1
    )
    pulled = jnp.dot(wide, flat, precision=HIGHEST, preferred_element_type=F32)
    routed = select(route, split3(jnp.concatenate([pulled, precision], axis=1)))
    pack[:, 0:16, :] = routed[:, 0:128].reshape(TILES, 16, 128)
    pack[:, 16:32, :] = routed[:, 128:256].reshape(TILES, 16, 128)
    pf[...] = pin[...].astype(F32)

    away = jnp.where((y == 0) & (z < 2), 3, 4)
    pl.semaphore_wait(pltpu.get_barrier_semaphore(), TILES - 1 + 1 + 15 + away)

    for d in AROUND:
        peer = lax.rem(t + d, TILES)
        remote(clon_ref.at[(peer,) + piece], coef.at[(0, t) + piece], 0, m, peer).start()
        remote(clat_ref.at[(peer,) + piece], coef.at[(1, t) + piece], 0, m, peer).start()
    for d in AROUND:
        peer = lax.rem(t + d, TILES)
        pltpu.make_async_remote_copy(
            src_ref=pack.at[peer], dst_ref=lists.at[c, t],
            send_sem=snd.at[1], recv_sem=list_rcv.at[d],
            device_id=(m, peer), device_id_type=MESH,
        ).start()
        remote(names.at[peer], named_in.at[c, t], NAMES, m, peer).start()
    own_o = [
        pltpu.make_async_copy(pack.at[t], lists.at[c, t], loc_sem.at[5]),
        pltpu.make_async_copy(names.at[t], named_in.at[c, t], loc_sem.at[13]),
    ]
    for copy in own_o:
        copy.start()
    for d in AROUND:
        peer = lax.rem(t + d, TILES)
        remote(w_ref.at[0, peer], wbuf.at[t], 2, m, peer).start()
    own[0].wait()
    own[1].wait()
    got(rs.at[pl.ds(0, 7)], 0)
    part = coef.at[(slice(None), slice(None)) + piece]
    for d in (2, 1, 3):
        remote(part, part, 4, lax.rem(y + d, 4) * 8 + z * 2 + c, t).start()

    for copy in own_o:
        copy.wait()
    remote(lists.at[c, t], lists.at[c, t], 5, sib, t).start()
    for d in (4, 2, 6, 7, 1, 3, 5):
        source = lax.rem(t + TILES - d, TILES)
        block = lists.at[c, source]
        pltpu.make_async_copy(block, block, list_rcv.at[d]).wait()
        remote(block, block, 5, sib, t).start()

    for d in AROUND:
        peer = lax.rem(t + d, TILES)
        remote(pf.at[peer], pbuf.at[t], 3, m, peer).start()
    own_p = pltpu.make_async_copy(pf.at[t], pbuf.at[t], loc_sem.at[4])
    own_p.start()

    got(names.at[pl.ds(0, 7)], NAMES)
    remote(named_in.at[c], named_in.at[c], NAMES + 1, sib, t).start()

    got(lists.at[0], 5)
    got(named_in.at[0], NAMES + 1)

    rows = lists[...].reshape(2 * TILES, 32, 128)
    pulled_parts = split3(rows[:, 0:16].reshape(256, 128))
    weight_parts = split3(rows[:, 16:32].reshape(256, 128))
    source = lax.broadcasted_iota(jnp.int32, (TILES, 128), 0)
    of_source = source == lax.broadcasted_iota(jnp.int32, (TILES, 128), 1) // 16

    def along(which):
        halves = [
            jnp.sum(jnp.where(of_source, named_in[core, :, which], 0.0), axis=0, keepdims=True)
            for core in range(2)
        ]
        return jnp.concatenate(halves, axis=1)

    seg_row = along(0)
    key_row = seg_row + 512.0 * along(1)
    row = lax.broadcasted_iota(jnp.int32, (256, 256), 0)
    fixed = lax.rem(row, 16) * 4 + 2 * c + lax.rem(row // 32, 2)
    for d in (2, 1, 3, 0):
        there = lax.rem(y + d, 4)
        level = lax.rem(t - 2 * there - lax.rem(row // 16, 2) + TILES, TILES)
        cell = fixed + level * 64
        each = select(
            (key_row == (cell + (row // 64) * 512).astype(F32)).astype(F32), weight_parts
        ).reshape(kinds, 2, 2, 16, 128)
        every = select(
            (seg_row == cell[0:64].astype(F32)).astype(F32), pulled_parts
        ).reshape(2, 2, 16, 128)
        for b in range(2):
            span = pl.ds(b * 128, 128)
            for near in range(2):
                ad[d, near, 0:kinds, :, span] = each[:, b, near]
                ad[d, near, kinds, :, span] = every[b, near]
        if d:
            remote(ad.at[d, 0], ybuf.at[0, d - 1], 7, there * 8 + z * 2 + c, t).start()
    for d in (2, 1, 3):
        there = lax.rem(y + d, 4)
        remote(ad.at[d, 1], ybuf.at[1, d - 1], 17, there * 8 + z * 2 + c, t).start()

    got(wbuf.at[pl.ds(0, 6)], 4)
    rows8 = coef.at[:, :, piece[0], :]
    remote(rows8, rows8, 6, sib, t).start()

    got(rows8, 6)
    retain[...] = 1.0 - 2.0 * coef[0] - 2.0 * coef[1]

    own[2].wait()
    got(pf.at[pl.ds(0, 7)], 2)

    top = lax.broadcasted_iota(jnp.int32, (8, 512), 0) == 0
    bottom = lax.broadcasted_iota(jnp.int32, (8, 512), 0) == 7
    nothing = jnp.zeros((8, 512), F32)

    def block_of(i):
        return i // 2, pl.ds((i % 2) * 8, 8)

    def sweep(step, carry):
        here = wbuf[block_of(0)]
        down_before, up = nothing, pltpu.roll(here, 7, 0)
        for i in range(16):
            place = block_of(i)
            after = wbuf[block_of(i + 1)] if i < 15 else nothing
            down = pltpu.roll(here, 1, 0)
            up_after = pltpu.roll(after, 7, 0)
            across = jnp.where(top, down_before, down) + jnp.where(bottom, up_after, up)
            zonal = pltpu.roll(here, 1, 1) + pltpu.roll(here, 511, 1)
            wbuf[place] = (
                retain[place] * here + coef[(0,) + place] * zonal + coef[(1,) + place] * across
            )
            here, down_before, up = after, down, up_after
        return carry

    lax.fori_loop(0, SWEEPS, sweep, 0, unroll=4)
    def pass_on(near, sem):
        got(ybuf.at[near], sem)
        s2[near] = ad[0, near] + ybuf[near, 0] + ybuf[near, 1] + ybuf[near, 2]
        level_to = lax.rem(t - 2 * y - near + TILES, TILES)
        for b in range(2):
            tz = 2 * near + b
            block = s2.at[near, :, :, pl.ds(b * 128, 128)]
            self = (level_to == t) & (z == tz)

            @pl.when(self)
            def _(block=block):
                pltpu.make_async_copy(block, zbuf.at[z], rcv.at[10]).start()

            @pl.when(jnp.logical_not(self))
            def _(block=block, tz=tz):
                remote(block, zbuf.at[z], 10, y * 8 + tz * 2 + c, level_to).start()

    own_p.wait()
    got(pbuf.at[pl.ds(0, 7)], 3)
    prod[...] = wbuf[...] * pbuf[...]
    mine = aligned(c, 256)
    remote(prod.at[:, :, aligned(1 - c, 256)], sibp, 8, sib, t).start()

    pass_on(0, 7)
    got(sibp, 8)
    for near in range(8):
        tile_to = lax.rem(near + t, TILES)
        half[near] = prod[tile_to, :, mine] + sibp[tile_to]
    for d in (2, 1, 3):
        there = lax.rem(y + d, 4)
        remote(half.at[pl.ds(2 * there, 2)], rsy.at[d - 1], 9, there * 8 + z * 2 + c, t).start()

    pass_on(1, 17)

    got(rsy, 9)
    sumy[...] = half[pl.ds(2 * y, 2)] + rsy[0] + rsy[1] + rsy[2]
    for d in (2, 1, 3):
        tz = lax.rem(z + d, 4)
        remote(
            sumy.at[tz // 2, :, aligned(lax.rem(tz, 2), 128)], rsz.at[d - 1], 18,
            y * 8 + tz * 2 + c, t,
        ).start()
    got(rsz, 18)
    total = sumy[z // 2, :, aligned(lax.rem(z, 2), 128)] + rsz[0] + rsz[1] + rsz[2]
    inc_red[...] = total

    got(zbuf, 10)
    normal = zbuf[0] + zbuf[1] + zbuf[2] + zbuf[3]
    images = lax.dot_general(
        total * scale, flat, (((1,), (1,)), ((), ())), precision=HIGHEST, preferred_element_type=F32
    )
    images = images * jnp.concatenate([normal[k] for k in range(kinds)], axis=1)
    adjoint = jnp.dot(images, flat, precision=HIGHEST, preferred_element_type=F32) - normal[kinds]
    adj_red[...] = adjoint


    def spread(d, carry):
        there = lax.rem(place16 + d, 16)
        remote(adj_red, fld.at[lead, :, cols], 11, 2 * there + c, t).start()
        return carry

    lax.fori_loop(1, 16, spread, 0)
    fld[lead, :, cols] = adjoint
    for d in (2, 1, 3):
        tz = lax.rem(z + d, 4)
        remote(inc_red, inc_ref.at[t, :, cols], 13, y * 8 + tz * 2 + c, lead).start()
    far = remote(inc_red, inc_ref.at[t, :, cols], 14, m, lead)

    @pl.when(lead == t)
    def _():
        pltpu.make_async_copy(inc_red, inc_ref.at[t, :, cols], rcv.at[14]).start()

    @pl.when(lead != t)
    def _():
        far.start()

    got(rs, 11)
    side = fld.at[:, :, mine]
    remote(side, side, 12, sib, t).start()

    got(side, 12)

    left(sibp, 8)
    prod[...] = fld[...] * pbuf[...]

    def sweep_back(step, carry):
        here = prod[block_of(0)]
        flux = coef[(1,) + block_of(0)] * here
        down_before, up = nothing, pltpu.roll(flux, 7, 0)
        for i in range(16):
            place = block_of(i)
            if i < 15:
                after = prod[block_of(i + 1)]
                flux_after = coef[(1,) + block_of(i + 1)] * after
            else:
                after = flux_after = nothing
            down = pltpu.roll(flux, 1, 0)
            up_after = pltpu.roll(flux_after, 7, 0)
            across = jnp.where(top, down_before, down) + jnp.where(bottom, up_after, up)
            flux_lon = coef[(0,) + place] * here
            prod[place] = (
                retain[place] * here
                + (pltpu.roll(flux_lon, 1, 1) + pltpu.roll(flux_lon, 511, 1))
                + across
            )
            here, flux, down_before, up = after, flux_after, down, up_after
        return carry

    lax.fori_loop(0, SWEEPS, sweep_back, 0, unroll=4)
    for d in AROUND:
        peer = lax.rem(t + d, TILES)
        remote(prod.at[peer], back_ref.at[t], 15, m, peer).start()
    own_b = pltpu.make_async_copy(prod.at[t], back_ref.at[t], loc_sem.at[6])
    own_b.start()

    got(rsz, 13)
    got(inc_red, 14)
    for near in range(2):
        block = inc_ref.at[lax.rem(t - 2 * y - near + TILES, TILES), :, mine]
        for d in (2, 1, 3):
            remote(block, block, 19, lax.rem(y + d, 4) * 8 + z * 2 + c, t).start()
    got(half.at[pl.ds(0, 6)], 19)
    side_inc = inc_ref.at[:, :, mine]
    remote(side_inc, side_inc, 16, sib, t).start()

    own_b.wait()
    got(prod.at[pl.ds(0, 7)], 15)
    got(side_inc, 16)
    left(rs.at[pl.ds(0, 7)], 0)
    left(pack.at[pl.ds(0, 7)], 1)
    left(wbuf.at[pl.ds(0, 7)], 2)
    left(pf.at[pl.ds(0, 7)], 3)
    left(wbuf.at[pl.ds(0, 6)], 4)
    left(lists.at[0], 5)
    left(names.at[pl.ds(0, 7)], NAMES)
    left(named_in.at[0], NAMES + 1)
    left(rows8, 6)
    left(ybuf.at[0], 7)
    left(ybuf.at[1], 17)
    left(rsy, 9)
    left(rsz, 18)

    @pl.when((y == 0) & (z < 2))
    def _():
        left(zbuf.at[pl.ds(0, 3)], 10)

    @pl.when((y > 0) | (z >= 2))
    def _():
        left(zbuf, 10)

    left(rs, 11)
    left(side, 12)
    left(rsz, 13)
    left(half.at[pl.ds(0, 6)], 19)

    @pl.when(lead != t)
    def _():
        far.wait_send()

    left(prod.at[pl.ds(0, 7)], 15)
    left(side_inc, 16)


def shards(
    weights, perturb, coef_lon, coef_lat, obs_value, obs_weight,
    obs_segment, obs_kind, obs_target, obs_count, operators,
):
    scale = 1.0 / math.sqrt(MEM)
    hbm = pl.BlockSpec(memory_space=pl.ANY)
    smem = pl.BlockSpec(memory_space=pltpu.SMEM)
    block = (TILES, 16, 512)
    dma = pltpu.SemaphoreType.DMA
    far = pl.BlockSpec(memory_space=pltpu.HBM)
    given = [
        pltpu.with_memory_space_constraint(a, pltpu.HBM)
        for a in (
            weights, perturb, coef_lon, coef_lat, obs_value, obs_weight,
            obs_segment.reshape(1, -1), obs_kind.reshape(1, -1), obs_target.reshape(1, -1), operators,
        )
    ]
    both = pl.pallas_call(
        kernel,
        out_shape=jax.ShapeDtypeStruct((2,) + block, F32),
        in_specs=[smem] + [far] * len(given),
        out_specs=hbm,
        scratch_shapes=[
            pltpu.VMEM(block, F32), pltpu.VMEM((2,) + block, F32),
            pltpu.VMEM(block, F32), pltpu.VMEM(block, F32), pltpu.VMEM(block, BF16),
            pltpu.VMEM(block, F32), pltpu.VMEM(obs_value.shape, F32),
            pltpu.VMEM(obs_weight.shape, F32), pltpu.VMEM(operators.shape, F32),
            pltpu.VMEM((1, obs_segment.shape[0]), jnp.int32),
            pltpu.VMEM((1, obs_kind.shape[0]), jnp.int32),
            pltpu.VMEM((1, obs_target.shape[0]), jnp.int32),
            pltpu.VMEM((TILES, 32, 128), F32), pltpu.VMEM((2, TILES, 32, 128), F32),
            pltpu.VMEM((TILES, 2, 128), F32), pltpu.VMEM((2, TILES, 2, 128), F32),
            pltpu.VMEM((4, 2, 5, 16, 256), F32), pltpu.VMEM((2, 3, 5, 16, 256), F32),
            pltpu.VMEM((2, 5, 16, 256), F32), pltpu.VMEM((4, 5, 16, 128), F32),
            pltpu.VMEM(block, F32), pltpu.VMEM((TILES, 16, 256), F32),
            pltpu.VMEM((TILES, 16, 256), F32), pltpu.VMEM((3, 2, 16, 256), F32),
            pltpu.VMEM((2, 16, 256), F32), pltpu.VMEM((3, 16, 128), F32),
            pltpu.VMEM((15, 16, 128), F32),
            pltpu.VMEM((16, 128), F32), pltpu.VMEM((16, 128), F32),
            pltpu.VMEM(block, F32),
            dma((14,)), dma((22,)), dma((22,)), dma((TILES,)),
        ],
        compiler_params=pltpu.CompilerParams(
            collective_id=0, has_side_effects=True, vmem_limit_bytes=VMEM_LIMIT
        ),
    )(obs_count, *given)
    return both[0] * scale, weights + (both[1] * scale)[None]


def solution(mesh):
    placed = (
        P("mem", None, "tile", None),
        P("mem", None, "tile", None),
        P(None, "tile", None),
        P(None, "tile", None),
        P(("mem", "tile"), None),
        P(("mem", "tile"), None),
        P(("mem", "tile")),
        P(("mem", "tile")),
        P(("mem", "tile"), None),
        P(("mem", "tile")),
        P(),
    )
    return jax.shard_map(
        shards,
        mesh=mesh,
        in_specs=placed,
        out_specs=(P(None, "tile", None), P("mem", None, "tile", None)),
        check_vma=False,
    )
```

```python
import math

import jax
import jax.numpy as jnp
from jax import lax
from jax.experimental import pallas as pl
from jax.experimental.pallas import tpu as pltpu
from jax.sharding import PartitionSpec as P

SWEEPS = 16
NAMES = 20
AROUND = (5, 3, 1, 7, 4, 2, 6)
VMEM_LIMIT = 24 * 1024 * 1024
MEM = 32
TILES = 8
MESH = pl.DeviceIdType.MESH
HIGHEST = lax.Precision.HIGHEST
F32 = jnp.float32
BF16 = jnp.bfloat16


def eye_mask(n):
    return lax.broadcasted_iota(jnp.int32, (n, n), 0) == lax.broadcasted_iota(jnp.int32, (n, n), 1)


def column(row):
    return jnp.sum(jnp.where(eye_mask(row.shape[1]), row, 0.0), axis=1, keepdims=True)


def as_row(col):
    return jnp.sum(jnp.where(eye_mask(col.shape[0]), col, 0.0), axis=0, keepdims=True)


def split3(x):
    hi = x.astype(BF16)
    rest = x - hi.astype(F32)
    mid = rest.astype(BF16)
    low = (rest - mid.astype(F32)).astype(BF16)
    return jnp.concatenate([hi, mid, low], axis=1)


def select(onehot, parts):
    width = parts.shape[1] // 3
    got = jnp.dot(onehot.astype(BF16), parts, preferred_element_type=F32)
    return got[:, 0:width] + got[:, width:2 * width] + got[:, 2 * width:3 * width]


def aligned(index, size):
    return pl.ds(pl.multiple_of(index * size, size), size)


def kernel(
    cnt_ref, w_ref, p_ref, clon_ref, clat_ref, ov_hbm, ow_hbm, seg_hbm, kind_hbm, tgt_hbm, op_hbm,
    both_ref,
    wbuf, coef, pbuf, pf, pin, retain, ov_ref, ow_ref, op_ref, seg_ref, kind_ref, tgt_ref,
    pack, lists, names, named_in, ad, ybuf, s2, zbuf, prod, sibp, half, rsy, sumy, rsz, rs, inc_red, adj_red, fld,
    loc_sem, snd, rcv, list_rcv,
):
    inc_ref, back_ref = both_ref.at[0], both_ref.at[1]
    m = lax.axis_index("mem")
    t = lax.axis_index("tile")
    y = m // 8
    z = lax.rem(m // 2, 4)
    c = lax.rem(m, 2)
    sib = m + 1 - 2 * c
    place16 = m // 2
    scale = 1.0 / math.sqrt(MEM)
    lead = lax.rem(2 * y + z // 2 + t, TILES)
    cols = aligned(2 * c + lax.rem(z, 2), 128)

    def remote(src, dst, sem, member, tile):
        return pltpu.make_async_remote_copy(
            src_ref=src, dst_ref=dst, send_sem=snd.at[sem], recv_sem=rcv.at[sem],
            device_id=(member, tile), device_id_type=MESH,
        )

    def got(ref, sem):
        pltpu.make_async_copy(ref, ref, rcv.at[sem]).wait()

    def left(ref, sem):
        pltpu.make_async_copy(ref, ref, snd.at[sem]).wait()

    def greet(member, tile):
        pl.semaphore_signal(
            pltpu.get_barrier_semaphore(), inc=1, device_id=(member, tile), device_id_type=MESH
        )

    for d in range(1, TILES):
        greet(m, lax.rem(t + d, TILES))
    greet(sib, t)

    def greet_core(d, carry):
        greet(2 * lax.rem(place16 + d, 16) + c, t)
        return carry

    lax.fori_loop(1, 16, greet_core, 0)
    for source in range(4):
        tile = lax.rem(t + 2 * y + z // 2, TILES)

        @pl.when((tile != t) | (z != source))
        def _(source=source, tile=tile):
            greet(y * 8 + source * 2 + c, tile)

    piece = (aligned(c, 8), aligned(y, 128))
    loads = [
        pltpu.make_async_copy(seg_hbm, seg_ref, loc_sem.at[10]),
        pltpu.make_async_copy(kind_hbm, kind_ref, loc_sem.at[11]),
        pltpu.make_async_copy(tgt_hbm, tgt_ref, loc_sem.at[12]),
        pltpu.make_async_copy(op_hbm, op_ref, loc_sem.at[7]),
        pltpu.make_async_copy(ov_hbm, ov_ref, loc_sem.at[8]),
        pltpu.make_async_copy(ow_hbm, ow_ref, loc_sem.at[9]),
        pltpu.make_async_copy(p_ref.at[0], pin, loc_sem.at[0]),
    ]
    own = [
        pltpu.make_async_copy(clon_ref.at[(t,) + piece], coef.at[(0, t) + piece], loc_sem.at[2]),
        pltpu.make_async_copy(clat_ref.at[(t,) + piece], coef.at[(1, t) + piece], loc_sem.at[3]),
        pltpu.make_async_copy(w_ref.at[0, t], wbuf.at[t], loc_sem.at[1]),
    ]
    for copy in loads + own:
        copy.start()

    slots = ov_ref.shape[0]
    kinds = op_ref.shape[0]
    live = lax.broadcasted_iota(jnp.int32, (slots, 1), 0) < cnt_ref[0]
    for copy in loads[:3]:
        copy.wait()
    target = tgt_ref[...].astype(F32)
    seg_row = seg_ref[...].astype(F32)
    kind_row = kind_ref[...].astype(F32)
    kind_col = column(kind_row)
    named = (
        target == lax.broadcasted_iota(jnp.int32, (TILES, slots), 0).astype(F32)
    ).astype(F32)
    upper = (
        lax.broadcasted_iota(jnp.int32, (slots, slots), 0)
        < lax.broadcasted_iota(jnp.int32, (slots, slots), 1)
    ).astype(F32)
    earlier = jnp.dot(named, upper, preferred_element_type=F32)
    rank = jnp.sum(earlier * named, axis=0, keepdims=True)
    place = target * 16.0 + rank
    at_lane = (
        column(rank) == lax.rem(lax.broadcasted_iota(jnp.int32, (slots, 128), 1), 16).astype(F32)
    ).astype(F32)
    told = jnp.dot(
        jnp.concatenate([named * seg_row, named * kind_row], axis=0), at_lane,
        precision=HIGHEST, preferred_element_type=F32,
    )
    for k in range(TILES):
        names[k, 0:1] = told[k:k + 1]
        names[k, 1:2] = told[TILES + k:TILES + k + 1]
    route = (
        lax.broadcasted_iota(jnp.int32, (128, slots), 0).astype(F32) == place
    ).astype(F32)
    for copy in loads[3:]:
        copy.wait()
    flat = op_ref[...].reshape(kinds * 128, 128)
    precision = jnp.where(live, ow_ref[...], 0.0)
    weighted = precision * ov_ref[...]
    wide = jnp.concatenate(
        [jnp.where(kind_col == float(k), weighted, 0.0) for k in range(kinds)], axis=1
    )
    pulled = jnp.dot(wide, flat, precision=HIGHEST, preferred_element_type=F32)
    routed = select(route, split3(jnp.concatenate([pulled, precision], axis=1)))
    pack[:, 0:16, :] = routed[:, 0:128].reshape(TILES, 16, 128)
    pack[:, 16:32, :] = routed[:, 128:256].reshape(TILES, 16, 128)
    pf[...] = pin[...].astype(F32)

    away = jnp.where((y == 0) & (z < 2), 3, 4)
    pl.semaphore_wait(pltpu.get_barrier_semaphore(), TILES - 1 + 1 + 15 + away)

    for d in AROUND:
        peer = lax.rem(t + d, TILES)
        remote(clon_ref.at[(peer,) + piece], coef.at[(0, t) + piece], 0, m, peer).start()
        remote(clat_ref.at[(peer,) + piece], coef.at[(1, t) + piece], 0, m, peer).start()
    for d in AROUND:
        peer = lax.rem(t + d, TILES)
        pltpu.make_async_remote_copy(
            src_ref=pack.at[peer], dst_ref=lists.at[c, t],
            send_sem=snd.at[1], recv_sem=list_rcv.at[d],
            device_id=(m, peer), device_id_type=MESH,
        ).start()
        remote(names.at[peer], named_in.at[c, t], NAMES, m, peer).start()
    own_o = [
        pltpu.make_async_copy(pack.at[t], lists.at[c, t], loc_sem.at[5]),
        pltpu.make_async_copy(names.at[t], named_in.at[c, t], loc_sem.at[13]),
    ]
    for copy in own_o:
        copy.start()
    for d in AROUND:
        peer = lax.rem(t + d, TILES)
        remote(w_ref.at[0, peer], wbuf.at[t], 2, m, peer).start()
    own[0].wait()
    own[1].wait()
    got(rs.at[pl.ds(0, 7)], 0)
    part = coef.at[(slice(None), slice(None)) + piece]
    for d in (2, 1, 3):
        remote(part, part, 4, lax.rem(y + d, 4) * 8 + z * 2 + c, t).start()

    for copy in own_o:
        copy.wait()
    remote(lists.at[c, t], lists.at[c, t], 5, sib, t).start()
    for d in (4, 2, 6, 7, 1, 3, 5):
        source = lax.rem(t + TILES - d, TILES)
        block = lists.at[c, source]
        pltpu.make_async_copy(block, block, list_rcv.at[d]).wait()
        remote(block, block, 5, sib, t).start()

    for d in AROUND:
        peer = lax.rem(t + d, TILES)
        remote(pf.at[peer], pbuf.at[t], 3, m, peer).start()
    own_p = pltpu.make_async_copy(pf.at[t], pbuf.at[t], loc_sem.at[4])
    own_p.start()

    got(names.at[pl.ds(0, 7)], NAMES)
    remote(named_in.at[c], named_in.at[c], NAMES + 1, sib, t).start()

    got(lists.at[0], 5)
    got(named_in.at[0], NAMES + 1)

    rows = lists[...].reshape(2 * TILES, 32, 128)
    pulled_parts = split3(rows[:, 0:16].reshape(256, 128))
    weight_parts = split3(rows[:, 16:32].reshape(256, 128))
    source = lax.broadcasted_iota(jnp.int32, (TILES, 128), 0)
    of_source = source == lax.broadcasted_iota(jnp.int32, (TILES, 128), 1) // 16

    def along(which):
        halves = [
            jnp.sum(jnp.where(of_source, named_in[core, :, which], 0.0), axis=0, keepdims=True)
            for core in range(2)
        ]
        return jnp.concatenate(halves, axis=1)

    seg_row = along(0)
    key_row = seg_row + 512.0 * along(1)
    row = lax.broadcasted_iota(jnp.int32, (256, 256), 0)
    fixed = lax.rem(row, 16) * 4 + 2 * c + lax.rem(row // 32, 2)
    for d in (2, 1, 3, 0):
        there = lax.rem(y + d, 4)
        level = lax.rem(t - 2 * there - lax.rem(row // 16, 2) + TILES, TILES)
        cell = fixed + level * 64
        each = select(
            (key_row == (cell + (row // 64) * 512).astype(F32)).astype(F32), weight_parts
        ).reshape(kinds, 2, 2, 16, 128)
        every = select(
            (seg_row == cell[0:64].astype(F32)).astype(F32), pulled_parts
        ).reshape(2, 2, 16, 128)
        for b in range(2):
            span = pl.ds(b * 128, 128)
            for near in range(2):
                ad[d, near, 0:kinds, :, span] = each[:, b, near]
                ad[d, near, kinds, :, span] = every[b, near]
        if d:
            remote(ad.at[d, 0], ybuf.at[0, d - 1], 7, there * 8 + z * 2 + c, t).start()
    for d in (2, 1, 3):
        there = lax.rem(y + d, 4)
        remote(ad.at[d, 1], ybuf.at[1, d - 1], 17, there * 8 + z * 2 + c, t).start()

    got(wbuf.at[pl.ds(0, 6)], 4)
    rows8 = coef.at[:, :, piece[0], :]
    remote(rows8, rows8, 6, sib, t).start()

    got(rows8, 6)
    retain[...] = 1.0 - 2.0 * coef[0] - 2.0 * coef[1]

    own[2].wait()
    got(pf.at[pl.ds(0, 7)], 2)

    top = lax.broadcasted_iota(jnp.int32, (8, 512), 0) == 0
    bottom = lax.broadcasted_iota(jnp.int32, (8, 512), 0) == 7
    nothing = jnp.zeros((8, 512), F32)

    def block_of(i):
        return i // 2, pl.ds((i % 2) * 8, 8)

    def sweep(step, carry):
        here = wbuf[block_of(0)]
        down_before, up = nothing, pltpu.roll(here, 7, 0)
        for i in range(16):
            place = block_of(i)
            after = wbuf[block_of(i + 1)] if i < 15 else nothing
            down = pltpu.roll(here, 1, 0)
            up_after = pltpu.roll(after, 7, 0)
            across = jnp.where(top, down_before, down) + jnp.where(bottom, up_after, up)
            zonal = pltpu.roll(here, 1, 1) + pltpu.roll(here, 511, 1)
            wbuf[place] = (
                retain[place] * here + coef[(0,) + place] * zonal + coef[(1,) + place] * across
            )
            here, down_before, up = after, down, up_after
        return carry

    lax.fori_loop(0, SWEEPS, sweep, 0, unroll=8)
    def pass_on(near, sem):
        got(ybuf.at[near], sem)
        s2[near] = ad[0, near] + ybuf[near, 0] + ybuf[near, 1] + ybuf[near, 2]
        level_to = lax.rem(t - 2 * y - near + TILES, TILES)
        for b in range(2):
            tz = 2 * near + b
            block = s2.at[near, :, :, pl.ds(b * 128, 128)]
            self = (level_to == t) & (z == tz)

            @pl.when(self)
            def _(block=block):
                pltpu.make_async_copy(block, zbuf.at[z], rcv.at[10]).start()

            @pl.when(jnp.logical_not(self))
            def _(block=block, tz=tz):
                remote(block, zbuf.at[z], 10, y * 8 + tz * 2 + c, level_to).start()

    own_p.wait()
    got(pbuf.at[pl.ds(0, 7)], 3)
    prod[...] = wbuf[...] * pbuf[...]
    mine = aligned(c, 256)
    remote(prod.at[:, :, aligned(1 - c, 256)], sibp, 8, sib, t).start()

    pass_on(0, 7)
    got(sibp, 8)
    for near in range(8):
        tile_to = lax.rem(near + t, TILES)
        half[near] = prod[tile_to, :, mine] + sibp[tile_to]
    for d in (2, 1, 3):
        there = lax.rem(y + d, 4)
        remote(half.at[pl.ds(2 * there, 2)], rsy.at[d - 1], 9, there * 8 + z * 2 + c, t).start()

    pass_on(1, 17)

    got(rsy, 9)
    sumy[...] = half[pl.ds(2 * y, 2)] + rsy[0] + rsy[1] + rsy[2]
    for d in (2, 1, 3):
        tz = lax.rem(z + d, 4)
        remote(
            sumy.at[tz // 2, :, aligned(lax.rem(tz, 2), 128)], rsz.at[d - 1], 18,
            y * 8 + tz * 2 + c, t,
        ).start()
    got(rsz, 18)
    total = sumy[z // 2, :, aligned(lax.rem(z, 2), 128)] + rsz[0] + rsz[1] + rsz[2]
    inc_red[...] = total

    got(zbuf, 10)
    normal = zbuf[0] + zbuf[1] + zbuf[2] + zbuf[3]
    images = lax.dot_general(
        total * scale, flat, (((1,), (1,)), ((), ())), precision=HIGHEST, preferred_element_type=F32
    )
    images = images * jnp.concatenate([normal[k] for k in range(kinds)], axis=1)
    adjoint = jnp.dot(images, flat, precision=HIGHEST, preferred_element_type=F32) - normal[kinds]
    adj_red[...] = adjoint


    def spread(d, carry):
        there = lax.rem(place16 + d, 16)
        remote(adj_red, fld.at[lead, :, cols], 11, 2 * there + c, t).start()
        return carry

    lax.fori_loop(1, 16, spread, 0)
    fld[lead, :, cols] = adjoint
    for d in (2, 1, 3):
        tz = lax.rem(z + d, 4)
        remote(inc_red, inc_ref.at[t, :, cols], 13, y * 8 + tz * 2 + c, lead).start()
    far = remote(inc_red, inc_ref.at[t, :, cols], 14, m, lead)

    @pl.when(lead == t)
    def _():
        pltpu.make_async_copy(inc_red, inc_ref.at[t, :, cols], rcv.at[14]).start()

    @pl.when(lead != t)
    def _():
        far.start()

    got(rs, 11)
    side = fld.at[:, :, mine]
    remote(side, side, 12, sib, t).start()

    got(side, 12)

    left(sibp, 8)
    prod[...] = fld[...] * pbuf[...]

    def sweep_back(step, carry):
        here = prod[block_of(0)]
        flux = coef[(1,) + block_of(0)] * here
        down_before, up = nothing, pltpu.roll(flux, 7, 0)
        for i in range(16):
            place = block_of(i)
            if i < 15:
                after = prod[block_of(i + 1)]
                flux_after = coef[(1,) + block_of(i + 1)] * after
            else:
                after = flux_after = nothing
            down = pltpu.roll(flux, 1, 0)
            up_after = pltpu.roll(flux_after, 7, 0)
            across = jnp.where(top, down_before, down) + jnp.where(bottom, up_after, up)
            flux_lon = coef[(0,) + place] * here
            prod[place] = (
                retain[place] * here
                + (pltpu.roll(flux_lon, 1, 1) + pltpu.roll(flux_lon, 511, 1))
                + across
            )
            here, flux, down_before, up = after, flux_after, down, up_after
        return carry

    lax.fori_loop(0, SWEEPS, sweep_back, 0, unroll=8)
    for d in AROUND:
        peer = lax.rem(t + d, TILES)
        remote(prod.at[peer], back_ref.at[t], 15, m, peer).start()
    own_b = pltpu.make_async_copy(prod.at[t], back_ref.at[t], loc_sem.at[6])
    own_b.start()

    got(rsz, 13)
    got(inc_red, 14)
    for near in range(2):
        block = inc_ref.at[lax.rem(t - 2 * y - near + TILES, TILES), :, mine]
        for d in (2, 1, 3):
            remote(block, block, 19, lax.rem(y + d, 4) * 8 + z * 2 + c, t).start()
    got(half.at[pl.ds(0, 6)], 19)
    side_inc = inc_ref.at[:, :, mine]
    remote(side_inc, side_inc, 16, sib, t).start()

    own_b.wait()
    got(prod.at[pl.ds(0, 7)], 15)
    got(side_inc, 16)
    left(rs.at[pl.ds(0, 7)], 0)
    left(pack.at[pl.ds(0, 7)], 1)
    left(wbuf.at[pl.ds(0, 7)], 2)
    left(pf.at[pl.ds(0, 7)], 3)
    left(wbuf.at[pl.ds(0, 6)], 4)
    left(lists.at[0], 5)
    left(names.at[pl.ds(0, 7)], NAMES)
    left(named_in.at[0], NAMES + 1)
    left(rows8, 6)
    left(ybuf.at[0], 7)
    left(ybuf.at[1], 17)
    left(rsy, 9)
    left(rsz, 18)

    @pl.when((y == 0) & (z < 2))
    def _():
        left(zbuf.at[pl.ds(0, 3)], 10)

    @pl.when((y > 0) | (z >= 2))
    def _():
        left(zbuf, 10)

    left(rs, 11)
    left(side, 12)
    left(rsz, 13)
    left(half.at[pl.ds(0, 6)], 19)

    @pl.when(lead != t)
    def _():
        far.wait_send()

    left(prod.at[pl.ds(0, 7)], 15)
    left(side_inc, 16)


def shards(
    weights, perturb, coef_lon, coef_lat, obs_value, obs_weight,
    obs_segment, obs_kind, obs_target, obs_count, operators,
):
    scale = 1.0 / math.sqrt(MEM)
    hbm = pl.BlockSpec(memory_space=pl.ANY)
    smem = pl.BlockSpec(memory_space=pltpu.SMEM)
    block = (TILES, 16, 512)
    dma = pltpu.SemaphoreType.DMA
    far = pl.BlockSpec(memory_space=pltpu.HBM)
    given = [
        pltpu.with_memory_space_constraint(a, pltpu.HBM)
        for a in (
            weights, perturb, coef_lon, coef_lat, obs_value, obs_weight,
            obs_segment.reshape(1, -1), obs_kind.reshape(1, -1), obs_target.reshape(1, -1), operators,
        )
    ]
    both = pl.pallas_call(
        kernel,
        out_shape=jax.ShapeDtypeStruct((2,) + block, F32),
        in_specs=[smem] + [far] * len(given),
        out_specs=hbm,
        scratch_shapes=[
            pltpu.VMEM(block, F32), pltpu.VMEM((2,) + block, F32),
            pltpu.VMEM(block, F32), pltpu.VMEM(block, F32), pltpu.VMEM(block, BF16),
            pltpu.VMEM(block, F32), pltpu.VMEM(obs_value.shape, F32),
            pltpu.VMEM(obs_weight.shape, F32), pltpu.VMEM(operators.shape, F32),
            pltpu.VMEM((1, obs_segment.shape[0]), jnp.int32),
            pltpu.VMEM((1, obs_kind.shape[0]), jnp.int32),
            pltpu.VMEM((1, obs_target.shape[0]), jnp.int32),
            pltpu.VMEM((TILES, 32, 128), F32), pltpu.VMEM((2, TILES, 32, 128), F32),
            pltpu.VMEM((TILES, 2, 128), F32), pltpu.VMEM((2, TILES, 2, 128), F32),
            pltpu.VMEM((4, 2, 5, 16, 256), F32), pltpu.VMEM((2, 3, 5, 16, 256), F32),
            pltpu.VMEM((2, 5, 16, 256), F32), pltpu.VMEM((4, 5, 16, 128), F32),
            pltpu.VMEM(block, F32), pltpu.VMEM((TILES, 16, 256), F32),
            pltpu.VMEM((TILES, 16, 256), F32), pltpu.VMEM((3, 2, 16, 256), F32),
            pltpu.VMEM((2, 16, 256), F32), pltpu.VMEM((3, 16, 128), F32),
            pltpu.VMEM((15, 16, 128), F32),
            pltpu.VMEM((16, 128), F32), pltpu.VMEM((16, 128), F32),
            pltpu.VMEM(block, F32),
            dma((14,)), dma((22,)), dma((22,)), dma((TILES,)),
        ],
        compiler_params=pltpu.CompilerParams(
            collective_id=0, has_side_effects=True, vmem_limit_bytes=VMEM_LIMIT
        ),
    )(obs_count, *given)
    return both[0] * scale, weights + (both[1] * scale)[None]


def solution(mesh):
    placed = (
        P("mem", None, "tile", None),
        P("mem", None, "tile", None),
        P(None, "tile", None),
        P(None, "tile", None),
        P(("mem", "tile"), None),
        P(("mem", "tile"), None),
        P(("mem", "tile")),
        P(("mem", "tile")),
        P(("mem", "tile"), None),
        P(("mem", "tile")),
        P(),
    )
    return jax.shard_map(
        shards,
        mesh=mesh,
        in_specs=placed,
        out_specs=(P(None, "tile", None), P("mem", None, "tile", None)),
        check_vma=False,
    )
```

```python
import math

import jax
import jax.numpy as jnp
from jax import lax
from jax.experimental import pallas as pl
from jax.experimental.pallas import tpu as pltpu
from jax.sharding import PartitionSpec as P

SWEEPS = 16
NAMES = 20
AROUND = (5, 3, 1, 7, 4, 2, 6)
VMEM_LIMIT = 24 * 1024 * 1024
MEM = 32
TILES = 8
MESH = pl.DeviceIdType.MESH
HIGHEST = lax.Precision.HIGHEST
F32 = jnp.float32
BF16 = jnp.bfloat16


def eye_mask(n):
    return lax.broadcasted_iota(jnp.int32, (n, n), 0) == lax.broadcasted_iota(jnp.int32, (n, n), 1)


def column(row):
    return jnp.sum(jnp.where(eye_mask(row.shape[1]), row, 0.0), axis=1, keepdims=True)


def as_row(col):
    return jnp.sum(jnp.where(eye_mask(col.shape[0]), col, 0.0), axis=0, keepdims=True)


def split3(x):
    hi = x.astype(BF16)
    rest = x - hi.astype(F32)
    mid = rest.astype(BF16)
    low = (rest - mid.astype(F32)).astype(BF16)
    return jnp.concatenate([hi, mid, low], axis=1)


def select(onehot, parts):
    width = parts.shape[1] // 3
    got = jnp.dot(onehot.astype(BF16), parts, preferred_element_type=F32)
    return got[:, 0:width] + got[:, width:2 * width] + got[:, 2 * width:3 * width]


def aligned(index, size):
    return pl.ds(pl.multiple_of(index * size, size), size)


def kernel(
    cnt_ref, w_ref, p_ref, clon_ref, clat_ref, ov_hbm, ow_hbm, seg_hbm, kind_hbm, tgt_hbm, op_hbm,
    both_ref,
    wbuf, coef, pbuf, pf, pin, retain, ov_ref, ow_ref, op_ref, seg_ref, kind_ref, tgt_ref,
    pack, lists, names, named_in, ad, ybuf, s2, zbuf, prod, sibp, half, rsy, sumy, rsz, rs, inc_red, adj_red, fld,
    loc_sem, snd, rcv, list_rcv,
):
    inc_ref, back_ref = both_ref.at[0], both_ref.at[1]
    m = lax.axis_index("mem")
    t = lax.axis_index("tile")
    y = m // 8
    z = lax.rem(m // 2, 4)
    c = lax.rem(m, 2)
    sib = m + 1 - 2 * c
    place16 = m // 2
    scale = 1.0 / math.sqrt(MEM)
    lead = lax.rem(2 * y + z // 2 + t, TILES)
    cols = aligned(2 * c + lax.rem(z, 2), 128)

    def remote(src, dst, sem, member, tile):
        return pltpu.make_async_remote_copy(
            src_ref=src, dst_ref=dst, send_sem=snd.at[sem], recv_sem=rcv.at[sem],
            device_id=(member, tile), device_id_type=MESH,
        )

    def got(ref, sem):
        pltpu.make_async_copy(ref, ref, rcv.at[sem]).wait()

    def left(ref, sem):
        pltpu.make_async_copy(ref, ref, snd.at[sem]).wait()

    def greet(member, tile):
        pl.semaphore_signal(
            pltpu.get_barrier_semaphore(), inc=1, device_id=(member, tile), device_id_type=MESH
        )

    for d in range(1, TILES):
        greet(m, lax.rem(t + d, TILES))
    greet(sib, t)

    def greet_core(d, carry):
        greet(2 * lax.rem(place16 + d, 16) + c, t)
        return carry

    lax.fori_loop(1, 16, greet_core, 0)
    for source in range(4):
        tile = lax.rem(t + 2 * y + z // 2, TILES)

        @pl.when((tile != t) | (z != source))
        def _(source=source, tile=tile):
            greet(y * 8 + source * 2 + c, tile)

    piece = (aligned(c, 8), aligned(y, 128))
    loads = [
        pltpu.make_async_copy(seg_hbm, seg_ref, loc_sem.at[10]),
        pltpu.make_async_copy(kind_hbm, kind_ref, loc_sem.at[11]),
        pltpu.make_async_copy(tgt_hbm, tgt_ref, loc_sem.at[12]),
        pltpu.make_async_copy(op_hbm, op_ref, loc_sem.at[7]),
        pltpu.make_async_copy(ov_hbm, ov_ref, loc_sem.at[8]),
        pltpu.make_async_copy(ow_hbm, ow_ref, loc_sem.at[9]),
        pltpu.make_async_copy(p_ref.at[0], pin, loc_sem.at[0]),
    ]
    own = [
        pltpu.make_async_copy(clon_ref.at[(t,) + piece], coef.at[(0, t) + piece], loc_sem.at[2]),
        pltpu.make_async_copy(clat_ref.at[(t,) + piece], coef.at[(1, t) + piece], loc_sem.at[3]),
        pltpu.make_async_copy(w_ref.at[0, t], wbuf.at[t], loc_sem.at[1]),
    ]
    for copy in loads + own:
        copy.start()

    slots = ov_ref.shape[0]
    kinds = op_ref.shape[0]
    live = lax.broadcasted_iota(jnp.int32, (slots, 1), 0) < cnt_ref[0]
    for copy in loads[:3]:
        copy.wait()
    target = tgt_ref[...].astype(F32)
    seg_row = seg_ref[...].astype(F32)
    kind_row = kind_ref[...].astype(F32)
    kind_col = column(kind_row)
    named = (
        target == lax.broadcasted_iota(jnp.int32, (TILES, slots), 0).astype(F32)
    ).astype(F32)
    upper = (
        lax.broadcasted_iota(jnp.int32, (slots, slots), 0)
        < lax.broadcasted_iota(jnp.int32, (slots, slots), 1)
    ).astype(F32)
    earlier = jnp.dot(named, upper, preferred_element_type=F32)
    rank = jnp.sum(earlier * named, axis=0, keepdims=True)
    place = target * 16.0 + rank
    at_lane = (
        column(rank) == lax.rem(lax.broadcasted_iota(jnp.int32, (slots, 128), 1), 16).astype(F32)
    ).astype(F32)
    told = jnp.dot(
        jnp.concatenate([named * seg_row, named * kind_row], axis=0), at_lane,
        precision=HIGHEST, preferred_element_type=F32,
    )
    for k in range(TILES):
        names[k, 0:1] = told[k:k + 1]
        names[k, 1:2] = told[TILES + k:TILES + k + 1]
    route = (
        lax.broadcasted_iota(jnp.int32, (128, slots), 0).astype(F32) == place
    ).astype(F32)
    for copy in loads[3:]:
        copy.wait()
    flat = op_ref[...].reshape(kinds * 128, 128)
    precision = jnp.where(live, ow_ref[...], 0.0)
    weighted = precision * ov_ref[...]
    wide = jnp.concatenate(
        [jnp.where(kind_col == float(k), weighted, 0.0) for k in range(kinds)], axis=1
    )
    pulled = jnp.dot(wide, flat, precision=HIGHEST, preferred_element_type=F32)
    routed = select(route, split3(jnp.concatenate([pulled, precision], axis=1)))
    pack[:, 0:16, :] = routed[:, 0:128].reshape(TILES, 16, 128)
    pack[:, 16:32, :] = routed[:, 128:256].reshape(TILES, 16, 128)
    pf[...] = pin[...].astype(F32)

    away = jnp.where((y == 0) & (z < 2), 3, 4)
    pl.semaphore_wait(pltpu.get_barrier_semaphore(), TILES - 1 + 1 + 15 + away)

    for d in AROUND:
        peer = lax.rem(t + d, TILES)
        remote(clon_ref.at[(peer,) + piece], coef.at[(0, t) + piece], 0, m, peer).start()
        remote(clat_ref.at[(peer,) + piece], coef.at[(1, t) + piece], 0, m, peer).start()
    for d in AROUND:
        peer = lax.rem(t + d, TILES)
        pltpu.make_async_remote_copy(
            src_ref=pack.at[peer], dst_ref=lists.at[c, t],
            send_sem=snd.at[1], recv_sem=list_rcv.at[d],
            device_id=(m, peer), device_id_type=MESH,
        ).start()
        remote(names.at[peer], named_in.at[c, t], NAMES, m, peer).start()
    own_o = [
        pltpu.make_async_copy(pack.at[t], lists.at[c, t], loc_sem.at[5]),
        pltpu.make_async_copy(names.at[t], named_in.at[c, t], loc_sem.at[13]),
    ]
    for copy in own_o:
        copy.start()
    for d in AROUND:
        peer = lax.rem(t + d, TILES)
        remote(w_ref.at[0, peer], wbuf.at[t], 2, m, peer).start()
    own[0].wait()
    own[1].wait()
    got(rs.at[pl.ds(0, 7)], 0)
    part = coef.at[(slice(None), slice(None)) + piece]
    for d in (2, 1, 3):
        remote(part, part, 4, lax.rem(y + d, 4) * 8 + z * 2 + c, t).start()

    for copy in own_o:
        copy.wait()
    remote(lists.at[c, t], lists.at[c, t], 5, sib, t).start()
    for d in (4, 2, 6, 7, 1, 3, 5):
        source = lax.rem(t + TILES - d, TILES)
        block = lists.at[c, source]
        pltpu.make_async_copy(block, block, list_rcv.at[d]).wait()
        remote(block, block, 5, sib, t).start()

    for d in AROUND:
        peer = lax.rem(t + d, TILES)
        remote(pf.at[peer], pbuf.at[t], 3, m, peer).start()
    own_p = pltpu.make_async_copy(pf.at[t], pbuf.at[t], loc_sem.at[4])
    own_p.start()

    got(names.at[pl.ds(0, 7)], NAMES)
    remote(named_in.at[c], named_in.at[c], NAMES + 1, sib, t).start()

    got(lists.at[0], 5)
    got(named_in.at[0], NAMES + 1)

    rows = lists[...].reshape(2 * TILES, 32, 128)
    pulled_parts = split3(rows[:, 0:16].reshape(256, 128))
    weight_parts = split3(rows[:, 16:32].reshape(256, 128))
    source = lax.broadcasted_iota(jnp.int32, (TILES, 128), 0)
    of_source = source == lax.broadcasted_iota(jnp.int32, (TILES, 128), 1) // 16

    def along(which):
        halves = [
            jnp.sum(jnp.where(of_source, named_in[core, :, which], 0.0), axis=0, keepdims=True)
            for core in range(2)
        ]
        return jnp.concatenate(halves, axis=1)

    seg_row = along(0)
    key_row = seg_row + 512.0 * along(1)
    row = lax.broadcasted_iota(jnp.int32, (256, 256), 0)
    fixed = lax.rem(row, 16) * 4 + 2 * c + lax.rem(row // 32, 2)
    for d in (2, 1, 3, 0):
        there = lax.rem(y + d, 4)
        level = lax.rem(t - 2 * there - lax.rem(row // 16, 2) + TILES, TILES)
        cell = fixed + level * 64
        each = select(
            (key_row == (cell + (row // 64) * 512).astype(F32)).astype(F32), weight_parts
        ).reshape(kinds, 2, 2, 16, 128)
        every = select(
            (seg_row == cell[0:64].astype(F32)).astype(F32), pulled_parts
        ).reshape(2, 2, 16, 128)
        for b in range(2):
            span = pl.ds(b * 128, 128)
            for near in range(2):
                ad[d, near, 0:kinds, :, span] = each[:, b, near]
                ad[d, near, kinds, :, span] = every[b, near]
        if d:
            remote(ad.at[d, 0], ybuf.at[0, d - 1], 7, there * 8 + z * 2 + c, t).start()
    for d in (2, 1, 3):
        there = lax.rem(y + d, 4)
        remote(ad.at[d, 1], ybuf.at[1, d - 1], 17, there * 8 + z * 2 + c, t).start()

    got(wbuf.at[pl.ds(0, 6)], 4)
    rows8 = coef.at[:, :, piece[0], :]
    remote(rows8, rows8, 6, sib, t).start()

    got(rows8, 6)
    retain[...] = 1.0 - 2.0 * coef[0] - 2.0 * coef[1]

    own[2].wait()
    got(pf.at[pl.ds(0, 7)], 2)

    top = lax.broadcasted_iota(jnp.int32, (8, 512), 0) == 0
    bottom = lax.broadcasted_iota(jnp.int32, (8, 512), 0) == 7
    nothing = jnp.zeros((8, 512), F32)

    def block_of(i):
        return i // 2, pl.ds((i % 2) * 8, 8)

    def sweep(step, carry):
        here = wbuf[block_of(0)]
        down_before, up = nothing, pltpu.roll(here, 7, 0)
        for i in range(16):
            place = block_of(i)
            after = wbuf[block_of(i + 1)] if i < 15 else nothing
            down = pltpu.roll(here, 1, 0)
            up_after = pltpu.roll(after, 7, 0)
            across = jnp.where(top, down_before, down) + jnp.where(bottom, up_after, up)
            zonal = pltpu.roll(here, 1, 1) + pltpu.roll(here, 511, 1)
            wbuf[place] = (
                retain[place] * here + coef[(0,) + place] * zonal + coef[(1,) + place] * across
            )
            here, down_before, up = after, down, up_after
        return carry

    lax.fori_loop(0, SWEEPS, sweep, 0, unroll=16)
    def pass_on(near, sem):
        got(ybuf.at[near], sem)
        s2[near] = ad[0, near] + ybuf[near, 0] + ybuf[near, 1] + ybuf[near, 2]
        level_to = lax.rem(t - 2 * y - near + TILES, TILES)
        for b in range(2):
            tz = 2 * near + b
            block = s2.at[near, :, :, pl.ds(b * 128, 128)]
            self = (level_to == t) & (z == tz)

            @pl.when(self)
            def _(block=block):
                pltpu.make_async_copy(block, zbuf.at[z], rcv.at[10]).start()

            @pl.when(jnp.logical_not(self))
            def _(block=block, tz=tz):
                remote(block, zbuf.at[z], 10, y * 8 + tz * 2 + c, level_to).start()

    own_p.wait()
    got(pbuf.at[pl.ds(0, 7)], 3)
    prod[...] = wbuf[...] * pbuf[...]
    mine = aligned(c, 256)
    remote(prod.at[:, :, aligned(1 - c, 256)], sibp, 8, sib, t).start()

    pass_on(0, 7)
    got(sibp, 8)
    for near in range(8):
        tile_to = lax.rem(near + t, TILES)
        half[near] = prod[tile_to, :, mine] + sibp[tile_to]
    for d in (2, 1, 3):
        there = lax.rem(y + d, 4)
        remote(half.at[pl.ds(2 * there, 2)], rsy.at[d - 1], 9, there * 8 + z * 2 + c, t).start()

    pass_on(1, 17)

    got(rsy, 9)
    sumy[...] = half[pl.ds(2 * y, 2)] + rsy[0] + rsy[1] + rsy[2]
    for d in (2, 1, 3):
        tz = lax.rem(z + d, 4)
        remote(
            sumy.at[tz // 2, :, aligned(lax.rem(tz, 2), 128)], rsz.at[d - 1], 18,
            y * 8 + tz * 2 + c, t,
        ).start()
    got(rsz, 18)
    total = sumy[z // 2, :, aligned(lax.rem(z, 2), 128)] + rsz[0] + rsz[1] + rsz[2]
    inc_red[...] = total

    got(zbuf, 10)
    normal = zbuf[0] + zbuf[1] + zbuf[2] + zbuf[3]
    images = lax.dot_general(
        total * scale, flat, (((1,), (1,)), ((), ())), precision=HIGHEST, preferred_element_type=F32
    )
    images = images * jnp.concatenate([normal[k] for k in range(kinds)], axis=1)
    adjoint = jnp.dot(images, flat, precision=HIGHEST, preferred_element_type=F32) - normal[kinds]
    adj_red[...] = adjoint


    def spread(d, carry):
        there = lax.rem(place16 + d, 16)
        remote(adj_red, fld.at[lead, :, cols], 11, 2 * there + c, t).start()
        return carry

    lax.fori_loop(1, 16, spread, 0)
    fld[lead, :, cols] = adjoint
    for d in (2, 1, 3):
        tz = lax.rem(z + d, 4)
        remote(inc_red, inc_ref.at[t, :, cols], 13, y * 8 + tz * 2 + c, lead).start()
    far = remote(inc_red, inc_ref.at[t, :, cols], 14, m, lead)

    @pl.when(lead == t)
    def _():
        pltpu.make_async_copy(inc_red, inc_ref.at[t, :, cols], rcv.at[14]).start()

    @pl.when(lead != t)
    def _():
        far.start()

    got(rs, 11)
    side = fld.at[:, :, mine]
    remote(side, side, 12, sib, t).start()

    got(side, 12)

    left(sibp, 8)
    prod[...] = fld[...] * pbuf[...]

    def sweep_back(step, carry):
        here = prod[block_of(0)]
        flux = coef[(1,) + block_of(0)] * here
        down_before, up = nothing, pltpu.roll(flux, 7, 0)
        for i in range(16):
            place = block_of(i)
            if i < 15:
                after = prod[block_of(i + 1)]
                flux_after = coef[(1,) + block_of(i + 1)] * after
            else:
                after = flux_after = nothing
            down = pltpu.roll(flux, 1, 0)
            up_after = pltpu.roll(flux_after, 7, 0)
            across = jnp.where(top, down_before, down) + jnp.where(bottom, up_after, up)
            flux_lon = coef[(0,) + place] * here
            prod[place] = (
                retain[place] * here
                + (pltpu.roll(flux_lon, 1, 1) + pltpu.roll(flux_lon, 511, 1))
                + across
            )
            here, flux, down_before, up = after, flux_after, down, up_after
        return carry

    lax.fori_loop(0, SWEEPS, sweep_back, 0, unroll=16)
    for d in AROUND:
        peer = lax.rem(t + d, TILES)
        remote(prod.at[peer], back_ref.at[t], 15, m, peer).start()
    own_b = pltpu.make_async_copy(prod.at[t], back_ref.at[t], loc_sem.at[6])
    own_b.start()

    got(rsz, 13)
    got(inc_red, 14)
    for near in range(2):
        block = inc_ref.at[lax.rem(t - 2 * y - near + TILES, TILES), :, mine]
        for d in (2, 1, 3):
            remote(block, block, 19, lax.rem(y + d, 4) * 8 + z * 2 + c, t).start()
    got(half.at[pl.ds(0, 6)], 19)
    side_inc = inc_ref.at[:, :, mine]
    remote(side_inc, side_inc, 16, sib, t).start()

    own_b.wait()
    got(prod.at[pl.ds(0, 7)], 15)
    got(side_inc, 16)
    left(rs.at[pl.ds(0, 7)], 0)
    left(pack.at[pl.ds(0, 7)], 1)
    left(wbuf.at[pl.ds(0, 7)], 2)
    left(pf.at[pl.ds(0, 7)], 3)
    left(wbuf.at[pl.ds(0, 6)], 4)
    left(lists.at[0], 5)
    left(names.at[pl.ds(0, 7)], NAMES)
    left(named_in.at[0], NAMES + 1)
    left(rows8, 6)
    left(ybuf.at[0], 7)
    left(ybuf.at[1], 17)
    left(rsy, 9)
    left(rsz, 18)

    @pl.when((y == 0) & (z < 2))
    def _():
        left(zbuf.at[pl.ds(0, 3)], 10)

    @pl.when((y > 0) | (z >= 2))
    def _():
        left(zbuf, 10)

    left(rs, 11)
    left(side, 12)
    left(rsz, 13)
    left(half.at[pl.ds(0, 6)], 19)

    @pl.when(lead != t)
    def _():
        far.wait_send()

    left(prod.at[pl.ds(0, 7)], 15)
    left(side_inc, 16)


def shards(
    weights, perturb, coef_lon, coef_lat, obs_value, obs_weight,
    obs_segment, obs_kind, obs_target, obs_count, operators,
):
    scale = 1.0 / math.sqrt(MEM)
    hbm = pl.BlockSpec(memory_space=pl.ANY)
    smem = pl.BlockSpec(memory_space=pltpu.SMEM)
    block = (TILES, 16, 512)
    dma = pltpu.SemaphoreType.DMA
    far = pl.BlockSpec(memory_space=pltpu.HBM)
    given = [
        pltpu.with_memory_space_constraint(a, pltpu.HBM)
        for a in (
            weights, perturb, coef_lon, coef_lat, obs_value, obs_weight,
            obs_segment.reshape(1, -1), obs_kind.reshape(1, -1), obs_target.reshape(1, -1), operators,
        )
    ]
    both = pl.pallas_call(
        kernel,
        out_shape=jax.ShapeDtypeStruct((2,) + block, F32),
        in_specs=[smem] + [far] * len(given),
        out_specs=hbm,
        scratch_shapes=[
            pltpu.VMEM(block, F32), pltpu.VMEM((2,) + block, F32),
            pltpu.VMEM(block, F32), pltpu.VMEM(block, F32), pltpu.VMEM(block, BF16),
            pltpu.VMEM(block, F32), pltpu.VMEM(obs_value.shape, F32),
            pltpu.VMEM(obs_weight.shape, F32), pltpu.VMEM(operators.shape, F32),
            pltpu.VMEM((1, obs_segment.shape[0]), jnp.int32),
            pltpu.VMEM((1, obs_kind.shape[0]), jnp.int32),
            pltpu.VMEM((1, obs_target.shape[0]), jnp.int32),
            pltpu.VMEM((TILES, 32, 128), F32), pltpu.VMEM((2, TILES, 32, 128), F32),
            pltpu.VMEM((TILES, 2, 128), F32), pltpu.VMEM((2, TILES, 2, 128), F32),
            pltpu.VMEM((4, 2, 5, 16, 256), F32), pltpu.VMEM((2, 3, 5, 16, 256), F32),
            pltpu.VMEM((2, 5, 16, 256), F32), pltpu.VMEM((4, 5, 16, 128), F32),
            pltpu.VMEM(block, F32), pltpu.VMEM((TILES, 16, 256), F32),
            pltpu.VMEM((TILES, 16, 256), F32), pltpu.VMEM((3, 2, 16, 256), F32),
            pltpu.VMEM((2, 16, 256), F32), pltpu.VMEM((3, 16, 128), F32),
            pltpu.VMEM((15, 16, 128), F32),
            pltpu.VMEM((16, 128), F32), pltpu.VMEM((16, 128), F32),
            pltpu.VMEM(block, F32),
            dma((14,)), dma((22,)), dma((22,)), dma((TILES,)),
        ],
        compiler_params=pltpu.CompilerParams(
            collective_id=0, has_side_effects=True, vmem_limit_bytes=VMEM_LIMIT
        ),
    )(obs_count, *given)
    return both[0] * scale, weights + (both[1] * scale)[None]


def solution(mesh):
    placed = (
        P("mem", None, "tile", None),
        P("mem", None, "tile", None),
        P(None, "tile", None),
        P(None, "tile", None),
        P(("mem", "tile"), None),
        P(("mem", "tile"), None),
        P(("mem", "tile")),
        P(("mem", "tile")),
        P(("mem", "tile"), None),
        P(("mem", "tile")),
        P(),
    )
    return jax.shard_map(
        shards,
        mesh=mesh,
        in_specs=placed,
        out_specs=(P(None, "tile", None), P("mem", None, "tile", None)),
        check_vma=False,
    )
```
